32 devices in a mesh: req: 16 (over z, y, core), tp: 2 (over x).
Axes of the slice: x: 2, y: 2, z: 4, core: 2. Of those that a mesh axis runs over, the one named last changes fastest.
Arguments:
- attn_ctx: bfloat16 [1024, 4096], P('req', 'tp'), may hold values from -6 to 6
- o_weight: bfloat16 [4096, 2880], P('tp'), may hold values from -0.09375 to 0.09375
- o_bias: bfloat16 [2880], replicated, may hold values from -3 to 3
- residual: bfloat16 [1024, 2880], P(('req', 'tp')), may hold values from -6 to 6
- post_gain: bfloat16 [2880], replicated, may hold values from 0.5 to 1.5
- router_weight: bfloat16 [2880, 8], replicated, may hold values from -0.01953125 to 0.01953125
- router_bias: float32 [8], replicated, may hold values from -0.4 to 0.4
- routes: int32 [1024, 4], P('req'), may hold values from 0 to 7, all different within a row; in each aligned block of 32 rows (0 to 31, 32 to 63, ...) at most 32 rows name the same one
- gate_up_weight: bfloat16 [16, 2880, 2, 1440], P('req', None, None, 'tp'), may hold values from -0.25 to 0.25
- gate_up_bias: bfloat16 [16, 2, 1440], P('req', None, 'tp'), may hold values from -3 to 3
- down_weight: bfloat16 [16, 1440, 2880], P('req', 'tp'), may hold values from -0.0546875 to 0.0546875
- down_bias: bfloat16 [8, 2880], replicated, may hold values from -3 to 3
- next_gain: bfloat16 [2880], replicated, may hold values from 0.5 to 1.5
Outputs:
- hidden_state: bfloat16 [1024, 2880], P(('req', 'tp'))
- normed_out: bfloat16 [1024, 2880], P(('req', 'tp'))
The draws below stay inside these ranges and needn't reach their ends.
Inputs may be any that keep to these rules, and one draw needn't show every extreme that they name: `routes`: each row names 4 different experts. In each aligned block of 32 rows no expert is named by more than 32 rows, a bound that some block reaches.
All inputs are finite; a program needn't handle non-finite values.
Results may differ from the reference program's by a relative error of at most 0.017.
Values may be sent and summed in bfloat16 or wider, within the bound.
A program may use at most 128 MiB of HBM per device.

```python
import math
import jax
import jax.numpy as jnp
import numpy as np
from jax import lax

D = 2880
HEADS = 64
HEAD_DIM = 64
FF = 2880
TOP = 4
EXPERTS = 8
ROWS_DEV = 32
ROWS = 1024
CAP = 32
N_REQ = 16
N_TP = 2


def steps_of(key, dims, split, smallest, top_value):
    factor_of = 1.0
    for position, shards_of in split:
        heights = jax.random.uniform(jax.random.fold_in(jax.random.fold_in(key, 6), position), (shards_of,), jnp.float32, smallest / len(split), top_value / len(split))
        factor_of = factor_of * jnp.repeat(jnp.exp(heights), dims[position] // shards_of).reshape((-1,) + (1,) * (len(dims) - 1 - position))
    return factor_of


def shared_out(rng, own, number, rows, number_of, top, bound, lean):
    order = jax.random.permutation(rng, number_of)
    crowded, usual = shares(number_of, rows * top, bound, lean, True), shares(number_of, rows * top, bound, lean, False)
    places = jnp.arange(number_of)

    def named(tallies, offset_by):
        used = int((tallies > 0).sum())
        fixed = max(1, used // 4)
        moved = fixed + (places - fixed + offset_by * (used - fixed)) % max(1, number_of - fixed)
        return jnp.zeros((number_of,), jnp.int32).at[order[jnp.where(places < fixed, places, moved)]].set(jnp.asarray(tallies, jnp.int32))

    tallies = jnp.where(number % 4 == 0, named(crowded, number // 4), named(usual, number - number // 4 - 1))
    mixed = jax.random.permutation(jax.random.fold_in(own, 3), number_of)
    giver, sink = mixed[0:number_of // 2 * 2:2], mixed[1:number_of // 2 * 2:2]
    room = jnp.minimum(tallies[giver] - 1, bound - tallies[sink]) // 2
    room = jnp.where((giver == order[0]) | (sink == order[0]) | (tallies[sink] == 0), 0, jnp.maximum(room, 0))
    moved = jax.random.randint(jax.random.fold_in(own, 4), (number_of // 2,), 0, 1 << 20) % (room + 1)
    tallies = tallies.at[giver].add(-moved).at[sink].add(moved)
    labels = jnp.searchsorted(jnp.cumsum(tallies), jnp.arange(rows * top), side="right").astype(jnp.int32)
    grid = labels.reshape(top, rows).T
    grid = grid[jax.random.permutation(jax.random.fold_in(own, 1), rows)]
    offset_by = jax.random.randint(jax.random.fold_in(own, 2), (rows, 1), 0, top)
    return jnp.take_along_axis(grid, (jnp.arange(top)[None, :] + offset_by) % top, axis=1)


def shares(amount, total, bound, lean, full):
    loads = [(1 << 20) // math.isqrt(rank ** lean) + 1 for rank in range(1, amount + 1)]
    largest = bound if full else min(bound, max(-(-total // amount), total * loads[0] // sum(loads)))
    least = 1 if total - largest >= amount - 1 else 0
    counts, surplus = [largest] + [least] * (amount - 1), total - largest - least * (amount - 1)
    while surplus > 0:
        candidates = [i for i in range(1, amount) if counts[i] < largest] or [i for i in range(1, amount) if counts[i] < bound]
        mass, budget = sum([loads[i] for i in candidates]), surplus
        for i in candidates:
            more = min(bound - counts[i], max(1, budget * loads[i] // mass), surplus)
            counts[i] = counts[i] + more
            surplus = surplus - more
    return np.array(counts)


def noise(stream_key, extent, deviation, limit, shards=(), held_as=jnp.bfloat16):
    factor_of = steps_of(stream_key, extent, shards, -0.22, 0.18) if shards else 1.0
    drawn = jax.random.normal(stream_key, extent, jnp.float32) * deviation * factor_of
    return jnp.minimum(jnp.maximum(drawn, -limit), limit).astype(held_as)


def setup_inputs(seed: int = 0) -> dict:
    key_list = jax.random.split(jax.random.key(seed), 14)
    attn_ctx = noise(key_list[0], (ROWS, HEADS * HEAD_DIM), 1.0, 6.0, ((0, 16), (1, 2)))
    o_weight = noise(key_list[1], (HEADS * HEAD_DIM, D), (HEADS * HEAD_DIM) ** -0.5, 0.09375, ((0, 2),))
    o_bias = noise(key_list[2], (D,), 0.5, 3.0)
    residual = noise(key_list[3], (ROWS, D), 1.0, 6.0, ((0, 32),))
    post_gain = jnp.clip(1.0 + 0.1 * jax.random.normal(key_list[4], (D,), jnp.float32), 0.5, 1.5).astype(jnp.bfloat16)
    router_weight = noise(key_list[5], (D, EXPERTS), (D * 32) ** -0.5, 0.01953125)
    router_bias = jnp.clip(jax.random.uniform(key_list[6], (EXPERTS,), jnp.float32, -0.4, 0.4), -0.4, 0.4)
    routes_keys = jax.random.split(jax.random.fold_in(key_list[7], 1), ROWS // ROWS_DEV)
    routes_turns = jax.random.permutation(jax.random.fold_in(key_list[7], 3), ROWS // ROWS_DEV)
    routes = jax.vmap(lambda own, number: shared_out(jax.random.fold_in(key_list[7], 2), own, number, ROWS_DEV, EXPERTS, TOP, CAP, 2))(routes_keys, routes_turns).reshape((ROWS, TOP))
    gate_up_weight = noise(key_list[8], (2 * EXPERTS, D, 2, FF // 2), (D // 6) ** -0.5, 0.25, ((0, 16), (3, 2)))
    gate_up_bias = noise(key_list[9], (2 * EXPERTS, 2, FF // 2), 0.5, 3.0, ((0, 16), (2, 2)))
    down_weight = noise(key_list[10], (2 * EXPERTS, FF // 2, D), (FF * 4) ** -0.5, 0.0546875, ((0, 16), (1, 2)))
    down_bias = noise(key_list[11], (EXPERTS, D), 0.5, 3.0)
    next_gain = jnp.clip(1.0 + 0.1 * jax.random.normal(key_list[12], (D,), jnp.float32), 0.5, 1.5).astype(jnp.bfloat16)
    return dict(attn_ctx=attn_ctx, o_weight=o_weight, o_bias=o_bias, residual=residual, post_gain=post_gain, router_weight=router_weight, router_bias=router_bias, routes=routes, gate_up_weight=gate_up_weight, gate_up_bias=gate_up_bias, down_weight=down_weight, down_bias=down_bias, next_gain=next_gain)


def rms_norm(values, gain):
    scale = lax.rsqrt(lax.optimization_barrier(jnp.mean(values * values, axis=-1, keepdims=True)) + 1e-05)
    return values * scale * gain.astype(jnp.float32)

def reference(attn_ctx, o_weight, o_bias, residual, post_gain, router_weight, router_bias, routes, gate_up_weight, gate_up_bias, down_weight, down_bias, next_gain):
    proj = jnp.dot(attn_ctx, o_weight, preferred_element_type=jnp.float32)
    state = (residual.astype(jnp.float32) + proj + o_bias.astype(jnp.float32)).astype(jnp.bfloat16)
    normed = rms_norm(state.astype(jnp.float32), post_gain).astype(jnp.bfloat16)
    logits = jnp.dot(normed, router_weight, preferred_element_type=jnp.float32) + router_bias.astype(jnp.float32)
    picked = jnp.take_along_axis(logits, routes, axis=1)
    expo = jnp.exp(picked)
    weights = expo / lax.optimization_barrier(jnp.sum(expo, axis=1, keepdims=True))
    most_rows = N_REQ * N_TP * CAP
    half_width = FF // 2
    part_width = FF // (2 * N_TP)
    normed_f = normed.astype(jnp.float32)

    def one_expert(expert, total):
        hits = routes == expert
        row_weight = lax.optimization_barrier(jnp.sum(jnp.where(hits, weights, jnp.zeros_like(weights)), axis=1))
        hit_any = jnp.any(hits, axis=1)
        keys = jnp.where(hit_any, 0, 1).astype(jnp.int32)
        order = jnp.argsort(keys, stable=True)[:most_rows].astype(jnp.int32)
        rows = normed_f[order]
        start = (2 * expert).astype(jnp.int32)
        w_pair = lax.dynamic_slice_in_dim(gate_up_weight, start, 2, 0).astype(jnp.float32)
        b_pair = lax.dynamic_slice_in_dim(gate_up_bias, start, 2, 0).astype(jnp.float32)
        w_gate = jnp.transpose(w_pair[:, :, 0, :], (1, 0, 2)).reshape(D, FF)
        w_up = jnp.transpose(w_pair[:, :, 1, :], (1, 0, 2)).reshape(D, FF)
        gate = jnp.dot(rows, w_gate) + b_pair[:, 0, :].reshape(FF)
        upper = jnp.dot(rows, w_up) + b_pair[:, 1, :].reshape(FF)
        gate = jnp.minimum(gate, 7.0)
        upper = jnp.clip(upper, -7.0, 7.0)
        act = ((upper + 1.0) * gate * jax.nn.sigmoid(1.702 * gate)).astype(jnp.bfloat16)
        down_pair = lax.dynamic_slice_in_dim(down_weight, start, 2, 0).astype(jnp.float32)
        down_parts = down_pair.reshape(2 * N_TP, part_width, D)
        act_parts = act.astype(jnp.float32).reshape(most_rows, 2 * N_TP, part_width)
        parts = jnp.einsum('npf,pfd->pnd', act_parts, down_parts)
        parts = lax.optimization_barrier(parts.astype(jnp.bfloat16)).astype(jnp.float32)
        bias_row = lax.dynamic_slice_in_dim(down_bias, expert.astype(jnp.int32), 1, 0).astype(jnp.float32)
        expert_out = lax.optimization_barrier(jnp.sum(parts, axis=0)) + bias_row
        return total.at[order].add(expert_out * row_weight[order][:, None])
    mixed = lax.fori_loop(0, EXPERTS, one_expert, jnp.zeros((ROWS, D), jnp.float32))
    hidden_state = (state.astype(jnp.float32) + mixed).astype(jnp.bfloat16)
    normed_out = rms_norm(hidden_state.astype(jnp.float32), next_gain).astype(jnp.bfloat16)
    return (hidden_state, normed_out)
```

```python
import functools

import jax
import jax.numpy as jnp
from jax import lax
from jax.experimental import pallas as pl
from jax.experimental.pallas import tpu as pltpu
from jax.sharding import PartitionSpec as P


def rms_norm(values, gain):
    scale = lax.rsqrt(jnp.mean(values * values, axis=-1, keepdims=True) + 1e-05)
    return values * scale * gain.astype(jnp.float32)


def route_rows(state, route_ids, post_gain, router_weight, router_bias, experts):
    normed = rms_norm(state.astype(jnp.float32), post_gain).astype(jnp.bfloat16)
    logits = jnp.dot(normed, router_weight, preferred_element_type=jnp.float32) + router_bias
    onehot = (route_ids[:, :, None] == jnp.arange(experts, dtype=jnp.int32)[None, None, :]).astype(
        jnp.float32
    )
    picked = jnp.sum(onehot * logits[:, None, :], axis=2)
    expo = jnp.exp(picked)
    weights = expo / jnp.sum(expo, axis=1, keepdims=True)
    table = jnp.sum(onehot * weights[:, :, None], axis=1)
    return (normed, weights, table)


def slot_numbers(route_blocks, experts, capacity):
    onehot = (
        route_blocks[:, :, None] == jnp.arange(experts, dtype=jnp.int32)[None, None, :]
    ).astype(jnp.int32)
    earlier = jnp.tril(jnp.ones((onehot.shape[1],) * 2, jnp.float32), -1)
    ranks = jnp.einsum("pq,bqe->bpe", earlier, onehot.astype(jnp.float32)).astype(jnp.int32)
    slots = jnp.sum(ranks * onehot, axis=2)
    offsets = jnp.arange(route_blocks.shape[0], dtype=jnp.int32)[:, None] * capacity
    return slots + offsets


def place_rows(normed, targets, block, req_count, top_count):
    width = normed.shape[1]
    source = jnp.repeat(normed, top_count, axis=0)
    buffer = jnp.zeros((req_count * block, width), jnp.bfloat16)
    index = jnp.concatenate([targets, targets + block])
    buffer = buffer.at[index].set(jnp.concatenate([source, source], axis=0))
    return buffer.reshape(req_count, block, width)


def weigh_parts(flat, targets, block, weights, top_count):
    first = jnp.take(flat, targets, axis=0).astype(jnp.float32)
    second = jnp.take(flat, targets + block, axis=0).astype(jnp.float32)
    values = (first + second) * weights.reshape(-1)[:, None]
    return jnp.sum(values.reshape(-1, top_count, flat.shape[1]), axis=1)


def expert_apply(rows, gate_up_weight, gate_up_bias, down_weight):
    local_width = gate_up_weight.shape[3]
    weight_mat = gate_up_weight[0].reshape(gate_up_weight.shape[1], 2 * local_width)
    projected = jnp.dot(rows, weight_mat, preferred_element_type=jnp.float32)
    projected = projected + gate_up_bias[0].reshape(2 * local_width).astype(jnp.float32)
    gate = jnp.minimum(projected[:, :local_width], 7.0)
    upper = jnp.clip(projected[:, local_width:], -7.0, 7.0)
    act = ((upper + 1.0) * gate * jax.nn.sigmoid(1.702 * gate)).astype(jnp.bfloat16)
    return jnp.dot(act, down_weight[0], preferred_element_type=jnp.float32)


def peer(bits, stride_x):
    req, tp = lax.axis_index("req"), lax.axis_index("tp")
    for bit in (1, 2, 4, 8):
        if bits & bit:
            req = req + bit * (1 - 2 * ((req // bit) % 2))
    return {"req": req, "tp": 1 - tp if stride_x else tp}


GATHER_WIDE = (1,)
SUM_WIDE = (1,)
PLAN = (
    "pre", "own", "ownb", "bias", "ry0", "rx0", "z1", "s1", "wz1", "rd0", "z2", "dd0", "s2",
    "rx1", "w0", "w1", "up00", "up01", "ry1", "up02", "wd1", "ry2", "dn00", "dn01", "rx2",
    "dn02", "dn03", "wc1", "z3", "rd1", "s3", "dd1", "up10", "up11", "up12", "rd2", "dn10",
    "dn11", "dn12", "dn13", "cs1", "dd2", "up20", "rx3", "ry3", "up21", "up22", "cs0", "ca1",
    "dn20", "dn21", "dn22", "rd3", "dn23", "cs2", "dd3", "ca2", "up30", "up31", "ha2", "up32",
    "dn30", "dn31", "dn32", "dn33", "ha1", "cs3", "ca3", "fa2", "ha3", "za1", "fa3", "ca0",
    "zt2", "zt1", "ha0", "zt3", "fin",
)


def layer_kernel(
    rows,
    width,
    experts,
    attn_hbm,
    o_weight_ref,
    residual_hbm,
    vectors_hbm,
    router_hbm,
    router_bias_hbm,
    routes_hbm,
    gate_up_ref,
    bias_hbm,
    down_ref,
    down_bias_hbm,
    hidden_ref,
    normed_ref,
    gathered,
    partial,
    core_in,
    half_in,
    full_in,
    layer_in,
    o_weight,
    gate_up,
    down,
    act,
    attn,
    proj,
    proj_out,
    proj_in,
    padded_rows,
    base,
    attn_ref,
    residual_ref,
    vectors_ref,
    router_ref,
    router_bias_ref,
    routes_ref,
    bias_ref,
    down_bias_ref,
    small_sems,
    load_sems,
    send_sems,
    recv_sems,
):
    half_rows = rows // 2
    hidden = down.shape[0]
    span = 8 * rows
    tail = width // 128 * 128
    req, tp = lax.axis_index("req"), lax.axis_index("tp")
    expert = req // 2
    step_width = 384
    steps = [(start, min(step_width, width - start)) for start in range(0, width, step_width)]
    links = {
        "x": (0, 1),
        "y": (2, 0),
        "c": (1, 0),
        "z1": (4, 0),
        "z2": (8, 0),
        "z3": (12, 0),
    }

    small = [
        pltpu.make_async_copy(source, target, small_sems.at[number])
        for number, (source, target) in enumerate(
            (
                (attn_hbm, attn_ref),
                (residual_hbm, residual_ref),
                (vectors_hbm, vectors_ref),
                (router_hbm, router_ref),
                (router_bias_hbm, router_bias_ref),
                (routes_hbm, routes_ref),
                (bias_hbm, bias_ref),
                (down_bias_hbm, down_bias_ref),
            )
        )
    ]
    small[0].start()
    loads = []
    for number, (start, size) in enumerate(steps):
        here = pl.ds(start, size)
        loads.append(
            pltpu.make_async_copy(o_weight_ref.at[here, :], o_weight.at[here, :], load_sems.at[number])
        )
    loads.append(pltpu.make_async_copy(gate_up_ref, gate_up, load_sems.at[len(steps)]))
    loads.append(pltpu.make_async_copy(down_ref, down, load_sems.at[len(steps) + 1]))
    for load in loads[:2] + small[1:] + loads[2:]:
        load.start()
    barrier = pltpu.get_barrier_semaphore()
    for link in links.values():
        pl.semaphore_signal(
            barrier, inc=1, device_id=peer(*link), device_id_type=pl.DeviceIdType.MESH
        )

    copies = {}

    def send(name, link, source, target):
        number = len(copies)
        copies[name] = pltpu.make_async_remote_copy(
            src_ref=source,
            dst_ref=target,
            send_sem=send_sems.at[number],
            recv_sem=recv_sems.at[number],
            device_id=peer(*links[link]),
            device_id_type=pl.DeviceIdType.MESH,
        )
        copies[name].start()

    def arrived(name):
        copies[name].wait_recv()

    def place(layer, core, spot, half=0):
        return ((layer * 2 + core) * 4 + spot) * rows + half * half_rows

    def block(ref, layer, core, spot):
        return ref.at[pl.ds(place(layer, core, spot), rows), :]

    def piece(ref, layer, core, spot, half):
        return ref.at[pl.ds(place(layer, core, spot, half), half_rows), :]

    small[0].wait()
    attn[0:rows, :] = attn_ref[pl.ds(pl.multiple_of(tp * rows, rows), rows), :]
    attn[rows:, :] = attn_ref[pl.ds(pl.multiple_of((1 - tp) * rows, rows), rows), :]
    for number, (start, size) in enumerate(steps):
        loads[number].wait()
        both = lax.dot_general(
            attn[...],
            o_weight[start : start + size, :],
            (((1,), (1,)), ((), ())),
            preferred_element_type=jnp.float32,
        )
        proj[:, start : start + size] = both[0:rows]
        proj_out[:, start : start + size] = both[rows:].astype(jnp.bfloat16)
        if number == 0:
            pl.semaphore_wait(barrier, len(links))
        here = pl.ds(start, size)
        send(("proj", number), "x", proj_out.at[:, here], proj_in.at[:, here])

    def op_pre():
        for load in small[1:]:
            load.wait()
        squares = jnp.zeros((rows, 1), jnp.float32)
        for number, (start, size) in enumerate(steps):
            here = slice(start, start + size)
            arrived(("proj", number))
            state = (
                residual_ref[:, here].astype(jnp.float32)
                + (proj[:, here] + proj_in[:, here].astype(jnp.float32))
                + vectors_ref[0:1, here]
            ).astype(jnp.bfloat16).astype(jnp.float32)
            base[:, here] = state
            squares = squares + jnp.sum(state * state, axis=1, keepdims=True)
        scale = lax.rsqrt(squares / width + 1e-05)
        padded_rows[:, tail:] = jnp.zeros((rows, padded_rows.shape[1] - tail), jnp.float32)
        padded_rows[:, 0:width] = base[...] * scale * vectors_ref[1:2, :]
        normed = padded_rows[:, 0:width].astype(jnp.bfloat16)
        logits = (
            lax.dot_general(
                normed,
                router_ref[...],
                (((1,), (1,)), ((), ())),
                preferred_element_type=jnp.float32,
            )
            + router_bias_ref[...]
        )
        given = routes_ref[...].astype(jnp.float32)
        here = (rows, given.shape[1])
        mine = lax.broadcasted_iota(jnp.int32, here, 0) + tp * rows
        mine = (mine == lax.broadcasted_iota(jnp.int32, here, 1)).astype(jnp.float32)
        routes = lax.dot_general(
            mine, given, (((1,), (1,)), ((), ())), preferred_element_type=jnp.float32
        )
        lane = lax.broadcasted_iota(jnp.int32, logits.shape, 1).astype(jnp.float32)
        hit = lane == routes[:, 0:1]
        for number in range(1, routes.shape[1]):
            hit = hit | (lane == routes[:, number : number + 1])
        expo = jnp.where(hit, jnp.exp(logits), 0.0)
        table = expo / jnp.sum(expo, axis=1, keepdims=True)
        high = table.astype(jnp.bfloat16).astype(jnp.float32)
        low = (table - high).astype(jnp.bfloat16).astype(jnp.float32)
        last = padded_rows[:, tail:]
        lane = lax.broadcasted_iota(jnp.int32, last.shape, 1) - (width - tail)
        for number in range(experts):
            last = jnp.where(lane == number, high[:, number : number + 1], last)
            last = jnp.where(lane == number + experts, low[:, number : number + 1], last)
        gathered[0:rows, 0:tail] = padded_rows[:, 0:tail].astype(jnp.bfloat16)
        gathered[0:rows, tail:] = last.astype(jnp.bfloat16)
        padded_rows[:, tail:] = last

    def op_bias():
        last = padded_rows[:, tail:]
        lane = lax.broadcasted_iota(jnp.int32, last.shape, 1) - (width - tail)
        for start, size in steps:
            here = slice(start, start + size)
            total = base[:, here]
            for number in range(experts):
                mine = (lane == number) | (lane == number + experts)
                weight = jnp.sum(jnp.where(mine, last, 0.0), axis=1, keepdims=True)
                total = total + weight * down_bias_ref[number : number + 1, here].astype(jnp.float32)
            base[:, here] = total

    def across(layer, spot):
        send(
            ("c", layer, spot),
            "c",
            block(gathered, layer, 0, spot),
            block(gathered, layer, 1, spot),
        )

    def along(name, link, layer, spot, half, far_layer, far_spot):
        send(
            name, link, piece(gathered, layer, 0, spot, half), piece(gathered, far_layer, 0, far_spot, half)
        )

    def spread(layer):
        if layer in GATHER_WIDE:
            along(("x", layer), "x", layer, 0, 1, layer, 1)
            along(("y", layer), "y", layer, 0, 0, layer, 2)
        else:
            own = block(gathered, layer, 0, 0)
            send(("x", layer), "x", own, block(gathered, layer, 0, 1))
            send(("y", layer), "y", own, block(gathered, layer, 0, 2))
        across(layer, 0)

    def op_own():
        own = block(gathered, 0, 0, 0)
        send("z1", "z1", own, block(gathered, 1, 0, 0))
        spread(0)

    def op_own2():
        send("z2", "z2", block(gathered, 0, 0, 0), block(gathered, 2, 0, 0))

    def op_z1():
        arrived("z1")

    def op_z2():
        arrived("z2")
        send("z3", "z1", block(gathered, 2, 0, 0), block(gathered, 3, 0, 0))

    def op_z3():
        arrived("z3")

    def op_rx(layer):
        arrived(("x", layer))
        if layer not in GATHER_WIDE:
            along(("yd", layer), "y", layer, 1, 1, layer, 3)
            across(layer, 1)

    def op_ry(layer):
        arrived(("y", layer))
        if layer not in GATHER_WIDE:
            along(("xd", layer), "x", layer, 2, 0, layer, 3)
            across(layer, 2)

    def op_wz(layer):
        source = layer - 1 if layer == 3 else 0
        link = "z1" if layer == 3 else "z" + str(layer)
        along(("zx", layer), link, source, 1, 0, layer, 1)
        along(("zy", layer), link, source, 2, 1, layer, 2)

    def op_wd(layer):
        arrived(("zx", layer))
        along(("yd", layer), "y", layer, 1, 0, layer, 3)
        arrived(("zy", layer))
        along(("xd", layer), "x", layer, 2, 1, layer, 3)

    def op_wc(layer):
        across(layer, 1)
        across(layer, 2)

    def op_rd(layer):
        arrived(("xd", layer))
        arrived(("yd", layer))
        across(layer, 3)

    def op_dd(layer):
        for spot in range(4):
            arrived(("c", layer, spot))

    def op_w(number):
        loads[len(steps) + number].wait()

    def op_up(layer, step):
        here = pl.ds(layer * span, span)
        start = step * 256
        size = min(256, hidden - start)
        sides = []
        for side in range(2):
            sides.append(
                lax.dot_general(
                    gathered[here, 0:width],
                    gate_up[pl.ds(side * hidden + start, size), :],
                    (((1,), (1,)), ((), ())),
                    preferred_element_type=jnp.float32,
                )
                + bias_ref[side : side + 1, start : start + size].astype(jnp.float32)
            )
        gate = jnp.minimum(sides[0], 7.0)
        upper = jnp.clip(sides[1], -7.0, 7.0)
        act[:, start : start + size] = (
            (upper + 1.0) * gate * jax.nn.sigmoid(1.702 * gate)
        ).astype(jnp.bfloat16)

    def op_dn(layer, step):
        here = pl.ds(layer * span, span)
        extra = gathered[here, tail:].astype(jnp.float32)
        lane = lax.broadcasted_iota(jnp.int32, extra.shape, 1) - (width - tail)
        mine = (lane == expert) | (lane == expert + experts)
        share = jnp.sum(jnp.where(mine, extra, 0.0), axis=1, keepdims=True)
        start = step * 768
        size = min(768, width - start)
        partial[here, start : start + size] = (
            jnp.dot(act[...], down[:, start : start + size], preferred_element_type=jnp.float32)
            * share
        ).astype(jnp.bfloat16)

    def op_cs(layer):
        send(
            ("cs", layer),
            "c",
            partial.at[pl.ds(place(layer, 1, 0), 4 * rows), :],
            core_in.at[pl.ds(layer * 4 * rows, 4 * rows), :],
        )

    def add(start, size, *others):
        total = partial[start : start + size, :].astype(jnp.float32)
        for other, first in others:
            total = total + other[first : first + size, :].astype(jnp.float32)
        partial[start : start + size, :] = total.astype(jnp.bfloat16)

    def half_place(layer, side, turn):
        return ((layer * 2 + side) * 2 + turn) * half_rows

    def send_half(layer, side, spot, half, turn):
        send(
            ("xy"[side] + "h", layer, turn),
            "xy"[side],
            piece(partial, layer, 0, spot, half),
            half_in.at[pl.ds(half_place(layer, side, turn), half_rows), :],
        )

    def add_half(layer, side, spot, half, turn):
        arrived(("xy"[side] + "h", layer, turn))
        add(place(layer, 0, spot, half), half_rows, (half_in, half_place(layer, side, turn)))

    def op_ca(layer):
        arrived(("cs", layer))
        first = layer * 4 * rows
        wide = layer in SUM_WIDE
        add(place(layer, 0, 3), rows, (core_in, first + 3 * rows))
        if wide:
            send_half(layer, 0, 3, 1, 0)
            send_half(layer, 1, 3, 0, 0)
        else:
            send_half(layer, 0, 3, 0, 0)
            send_half(layer, 1, 3, 1, 0)
        for spot in (1, 2):
            add(place(layer, 0, spot), rows, (core_in, first + spot * rows))
            if wide:
                send_half(layer, spot - 1, spot, 2 - spot, 1)
        add(place(layer, 0, 0), rows, (core_in, first))

    def op_ha(layer):
        if layer in SUM_WIDE:
            add_half(layer, 0, 2, 1, 0)
            add_half(layer, 1, 1, 0, 0)
            add_half(layer, 0, 0, 1, 1)
            add_half(layer, 1, 0, 0, 1)
            for part, (spot, half, size) in enumerate(((1, 0, 1), (2, 1, 1), (0, 0, 2))):
                send(
                    ("zs", layer, part),
                    "z" + str(layer),
                    partial.at[pl.ds(place(layer, 0, spot, half), size * half_rows), :],
                    layer_in.at[
                        pl.ds((layer * 2 - 2) * rows + part * half_rows, size * half_rows), :
                    ],
                )
            return
        add_half(layer, 0, 2, 0, 0)
        add_half(layer, 1, 1, 1, 0)
        for side, link in enumerate("xy"):
            send(
                (link + "f", layer),
                link,
                block(partial, layer, 0, 1 + side),
                full_in.at[pl.ds((layer * 2 + side) * rows, rows), :],
            )

    def op_fa(layer):
        first = layer * 2 * rows
        arrived(("xf", layer))
        arrived(("yf", layer))
        add(place(layer, 0, 0), rows, (full_in, first), (full_in, first + rows))
        send(
            ("zs", layer, 2),
            "z" + str(layer),
            block(partial, layer, 0, 0),
            layer_in.at[pl.ds((layer * 2 - 1) * rows, rows), :],
        )

    def op_za(layer):
        first = (layer * 2 - 2) * rows
        arrived(("zs", layer, 0))
        add(place(0, 0, 1, 0), half_rows, (layer_in, first))
        arrived(("zs", layer, 1))
        add(place(0, 0, 2, 1), half_rows, (layer_in, first + half_rows))

    def op_zt(layer):
        first = (layer * 2 - 1) * rows
        arrived(("zs", layer, 2))
        base[...] += layer_in[first : first + rows, :].astype(jnp.float32)

    def op_fin():
        base[...] += partial[0:rows, :].astype(jnp.float32)
        arrived(("xf", 0))
        arrived(("yf", 0))
        total = base[...]
        for first in (0, rows):
            total = total + full_in[first : first + rows, :].astype(jnp.float32)
        total = total.astype(jnp.bfloat16)
        hidden_ref[...] = total
        total = total.astype(jnp.float32)
        scale = lax.rsqrt(jnp.sum(total * total, axis=1, keepdims=True) / width + 1e-05)
        normed_ref[...] = (total * scale * vectors_ref[2:3, :]).astype(jnp.bfloat16)

    ops = dict(
        pre=op_pre, bias=op_bias, own=op_own, ownb=op_own2, w=op_w, z1=op_z1, z2=op_z2, z3=op_z3,
        s=spread, rx=op_rx, ry=op_ry, wz=op_wz, wd=op_wd, wc=op_wc, rd=op_rd, dd=op_dd, up=op_up,
        dn=op_dn, cs=op_cs, ca=op_ca, ha=op_ha, fa=op_fa, za=op_za, zt=op_zt, fin=op_fin,
    )
    for name in PLAN:
        if name in ops:
            ops[name]()
        else:
            stem = name.rstrip("0123456789")
            ops[stem](*[int(digit) for digit in name[len(stem) :]])
    for copy in copies.values():
        copy.wait_send()


def whole_layer(
    attn_ctx,
    o_weight,
    o_bias,
    residual,
    post_gain,
    router_weight,
    router_bias,
    routes,
    gate_up_weight,
    gate_up_bias,
    down_weight,
    down_bias,
    next_gain,
):
    rows, width = residual.shape
    experts = router_bias.shape[0]
    hidden = down_weight.shape[1]
    padded = (width + 2 * experts + 127) // 128 * 128
    gate_up = jnp.transpose(gate_up_weight[0], (1, 2, 0)).reshape(2 * hidden, width)
    bias = gate_up_bias[0]
    turn = lax.broadcasted_iota(jnp.int32, (3, width), 0)
    vectors = jnp.where(
        turn == 0, o_bias[None, :], jnp.where(turn == 1, post_gain[None, :], next_gain[None, :])
    ).astype(jnp.float32)
    vmem = pl.BlockSpec(memory_space=pltpu.VMEM)
    hbm = pl.BlockSpec(memory_space=pl.ANY)
    copies = 128
    out = jax.ShapeDtypeStruct((rows, width), jnp.bfloat16)
    return pl.pallas_call(
        functools.partial(layer_kernel, rows, width, experts),
        out_shape=(out, out),
        in_specs=[hbm] * 11,
        out_specs=(vmem, vmem),
        scratch_shapes=[
            pltpu.VMEM((32 * rows, padded), jnp.bfloat16),
            pltpu.VMEM((32 * rows, width), jnp.bfloat16),
            pltpu.VMEM((16 * rows, width), jnp.bfloat16),
            pltpu.VMEM((8 * rows, width), jnp.bfloat16),
            pltpu.VMEM((8 * rows, width), jnp.bfloat16),
            pltpu.VMEM((6 * rows, width), jnp.bfloat16),
            pltpu.VMEM((width, attn_ctx.shape[1]), jnp.bfloat16),
            pltpu.VMEM((2 * hidden, width), jnp.bfloat16),
            pltpu.VMEM((hidden, width), jnp.bfloat16),
            pltpu.VMEM((8 * rows, hidden), jnp.bfloat16),
            pltpu.VMEM(attn_ctx.shape, jnp.bfloat16),
            pltpu.VMEM((rows, width), jnp.float32),
            pltpu.VMEM((rows, width), jnp.bfloat16),
            pltpu.VMEM((rows, width), jnp.bfloat16),
            pltpu.VMEM((rows, padded), jnp.float32),
            pltpu.VMEM((rows, width), jnp.float32),
            pltpu.VMEM(attn_ctx.shape, jnp.bfloat16),
            pltpu.VMEM((rows, width), jnp.bfloat16),
            pltpu.VMEM((3, width), jnp.float32),
            pltpu.VMEM((experts, width), jnp.bfloat16),
            pltpu.VMEM((1, experts), jnp.float32),
            pltpu.VMEM(routes.shape[::-1], jnp.int32),
            pltpu.VMEM((2, hidden), jnp.bfloat16),
            pltpu.VMEM((experts, width), jnp.bfloat16),
            pltpu.SemaphoreType.DMA((8,)),
            pltpu.SemaphoreType.DMA((16,)),
            pltpu.SemaphoreType.DMA((copies,)),
            pltpu.SemaphoreType.DMA((copies,)),
        ],
        compiler_params=pltpu.CompilerParams(
            collective_id=0, has_side_effects=True, vmem_limit_bytes=60900 * 1024
        ),
    )(
        attn_ctx,
        o_weight.T,
        residual,
        vectors,
        router_weight.T,
        router_bias.reshape(1, experts),
        routes.T,
        gate_up,
        bias,
        down_weight[0],
        down_bias,
    )


def per_device(
    attn_ctx,
    o_weight,
    o_bias,
    residual,
    post_gain,
    router_weight,
    router_bias,
    routes,
    gate_up_weight,
    gate_up_bias,
    down_weight,
    down_bias,
    next_gain,
):
    req_count = lax.axis_size("req")
    tp_count = lax.axis_size("tp")
    width = o_weight.shape[1]
    tokens_here = attn_ctx.shape[0]
    own_rows = tokens_here // tp_count
    experts = req_count // 2
    top_count = routes.shape[1]
    capacity = min(own_rows, max(2, 2 * top_count * own_rows // experts))
    if capacity == own_rows and req_count == 16 and tp_count == 2 and own_rows % 32 == 0:
        return whole_layer(
            attn_ctx,
            o_weight,
            o_bias,
            residual,
            post_gain,
            router_weight,
            router_bias,
            routes,
            gate_up_weight,
            gate_up_bias,
            down_weight,
            down_bias,
            next_gain,
        )
    own_start = lax.axis_index("tp") * own_rows
    bias_vec = o_bias.astype(jnp.float32)
    proj = jnp.dot(attn_ctx, o_weight, preferred_element_type=jnp.float32).astype(jnp.bfloat16)
    if tp_count == 2:
        theirs = lax.dynamic_slice_in_dim(proj, own_rows - own_start, own_rows, 0)
        mine = lax.dynamic_slice_in_dim(proj, own_start, own_rows, 0)
        arrived = lax.ppermute(theirs, "tp", [(0, 1), (1, 0)])
        summed = mine.astype(jnp.float32) + arrived.astype(jnp.float32)
    else:
        summed = lax.psum_scatter(proj, "tp", scatter_dimension=0, tiled=True).astype(jnp.float32)
    state = (residual.astype(jnp.float32) + summed + bias_vec).astype(jnp.bfloat16)
    own_routes = lax.dynamic_slice_in_dim(routes, own_start, own_rows, 0)
    normed, weights, table = route_rows(
        state, own_routes, post_gain, router_weight, router_bias, experts
    )
    bias_terms = jnp.dot(table, down_bias.astype(jnp.float32), precision=lax.Precision.HIGHEST)
    slots = slot_numbers(own_routes.reshape(1, own_rows * top_count), experts, capacity)
    targets = 2 * own_routes.reshape(-1) * capacity + slots.reshape(-1)
    outgoing = place_rows(normed, targets, capacity, req_count, top_count)
    incoming = lax.all_to_all(outgoing, "req", split_axis=0, concat_axis=0, tiled=True)
    gathered = lax.all_gather(incoming[None], "tp", axis=0, tiled=True).reshape(-1, width)
    sums = lax.psum_scatter(
        expert_apply(gathered, gate_up_weight, gate_up_bias, down_weight).astype(jnp.bfloat16),
        "tp",
        scatter_dimension=0,
        tiled=True,
    ).astype(jnp.float32)
    returned = lax.all_to_all(
        sums.reshape(req_count, capacity, width).astype(jnp.bfloat16),
        "req",
        split_axis=0,
        concat_axis=0,
        tiled=True,
    ).astype(jnp.float32)
    mixed = weigh_parts(returned.reshape(-1, width), targets, capacity, weights, top_count)
    hidden_state = (state.astype(jnp.float32) + mixed + bias_terms).astype(jnp.bfloat16)
    normed_out = rms_norm(hidden_state.astype(jnp.float32), next_gain).astype(jnp.bfloat16)
    return (hidden_state, normed_out)


def solution(mesh):
    return jax.shard_map(
        per_device,
        mesh=mesh,
        in_specs=(
            P("req", "tp"),
            P("tp", None),
            P(),
            P(("req", "tp"), None),
            P(),
            P(),
            P(),
            P("req", None),
            P("req", None, None, "tp"),
            P("req", None, "tp"),
            P("req", "tp", None),
            P(),
            P(),
        ),
        out_specs=(P(("req", "tp"), None), P(("req", "tp"), None)),
        check_vma=False,
    )
```

```python
import functools

import jax
import jax.numpy as jnp
from jax import lax
from jax.experimental import pallas as pl
from jax.experimental.pallas import tpu as pltpu
from jax.sharding import PartitionSpec as P


def rms_norm(values, gain):
    scale = lax.rsqrt(jnp.mean(values * values, axis=-1, keepdims=True) + 1e-05)
    return values * scale * gain.astype(jnp.float32)


def route_rows(state, route_ids, post_gain, router_weight, router_bias, experts):
    normed = rms_norm(state.astype(jnp.float32), post_gain).astype(jnp.bfloat16)
    logits = jnp.dot(normed, router_weight, preferred_element_type=jnp.float32) + router_bias
    onehot = (route_ids[:, :, None] == jnp.arange(experts, dtype=jnp.int32)[None, None, :]).astype(
        jnp.float32
    )
    picked = jnp.sum(onehot * logits[:, None, :], axis=2)
    expo = jnp.exp(picked)
    weights = expo / jnp.sum(expo, axis=1, keepdims=True)
    table = jnp.sum(onehot * weights[:, :, None], axis=1)
    return (normed, weights, table)


def slot_numbers(route_blocks, experts, capacity):
    onehot = (
        route_blocks[:, :, None] == jnp.arange(experts, dtype=jnp.int32)[None, None, :]
    ).astype(jnp.int32)
    earlier = jnp.tril(jnp.ones((onehot.shape[1],) * 2, jnp.float32), -1)
    ranks = jnp.einsum("pq,bqe->bpe", earlier, onehot.astype(jnp.float32)).astype(jnp.int32)
    slots = jnp.sum(ranks * onehot, axis=2)
    offsets = jnp.arange(route_blocks.shape[0], dtype=jnp.int32)[:, None] * capacity
    return slots + offsets


def place_rows(normed, targets, block, req_count, top_count):
    width = normed.shape[1]
    source = jnp.repeat(normed, top_count, axis=0)
    buffer = jnp.zeros((req_count * block, width), jnp.bfloat16)
    index = jnp.concatenate([targets, targets + block])
    buffer = buffer.at[index].set(jnp.concatenate([source, source], axis=0))
    return buffer.reshape(req_count, block, width)


def weigh_parts(flat, targets, block, weights, top_count):
    first = jnp.take(flat, targets, axis=0).astype(jnp.float32)
    second = jnp.take(flat, targets + block, axis=0).astype(jnp.float32)
    values = (first + second) * weights.reshape(-1)[:, None]
    return jnp.sum(values.reshape(-1, top_count, flat.shape[1]), axis=1)


def expert_apply(rows, gate_up_weight, gate_up_bias, down_weight):
    local_width = gate_up_weight.shape[3]
    weight_mat = gate_up_weight[0].reshape(gate_up_weight.shape[1], 2 * local_width)
    projected = jnp.dot(rows, weight_mat, preferred_element_type=jnp.float32)
    projected = projected + gate_up_bias[0].reshape(2 * local_width).astype(jnp.float32)
    gate = jnp.minimum(projected[:, :local_width], 7.0)
    upper = jnp.clip(projected[:, local_width:], -7.0, 7.0)
    act = ((upper + 1.0) * gate * jax.nn.sigmoid(1.702 * gate)).astype(jnp.bfloat16)
    return jnp.dot(act, down_weight[0], preferred_element_type=jnp.float32)


def peer(bits, stride_x):
    req, tp = lax.axis_index("req"), lax.axis_index("tp")
    for bit in (1, 2, 4, 8):
        if bits & bit:
            req = req + bit * (1 - 2 * ((req // bit) % 2))
    return {"req": req, "tp": 1 - tp if stride_x else tp}


GATHER_WIDE = (1,)
SUM_WIDE = (1,)
PLAN = (
    "pre", "own", "ownc", "bias", "ownb", "rx0", "ry0", "wz1", "rd0", "z1", "s1", "z2", "s2",
    "dd0", "wd1", "w0", "up00", "up01", "up02", "ry1", "w1", "dn00", "rx1", "ry2", "rx2",
    "wc1", "dn01", "dn02", "z3", "rd1", "s3", "dn03", "dd1", "up10", "up11", "up12", "rd2",
    "dn10", "dn11", "dn12", "dd2", "dn13", "cs10", "cs11", "up20", "rx3", "ry3", "up21",
    "up22", "ca10", "ca11", "dn20", "dn21", "dn22", "rd3", "dn23", "cs20", "dd3", "cs21",
    "up30", "ca20", "up31", "ca21", "ha10", "up32", "dn30", "ha20", "cs00", "za10", "ha21",
    "dn31", "dn32", "dn33", "cs30", "ha11", "cs31", "fa20", "ca30", "ca31", "fa21", "ha30",
    "ha31", "za11", "zt10", "fa30", "cs01", "zt20", "fa31", "ca00", "zt11", "ca01", "ha00",
    "ha01", "zt30", "zt31", "zt21", "fin",
)


def layer_kernel(
    rows,
    width,
    experts,
    attn_hbm,
    o_weight_ref,
    residual_hbm,
    o_bias_hbm,
    post_gain_hbm,
    next_gain_hbm,
    router_hbm,
    router_bias_hbm,
    routes_hbm,
    gate_up_ref,
    bias_hbm,
    down_ref,
    down_bias_hbm,
    out_ref,
    gathered,
    partial,
    core_in,
    half_in,
    full_in,
    layer_in,
    o_weight,
    gate_up,
    down,
    act,
    attn,
    proj,
    proj_out,
    proj_in,
    padded_rows,
    base,
    attn_ref,
    residual_ref,
    o_bias_ref,
    post_gain_ref,
    next_gain_ref,
    vectors_ref,
    router_ref,
    router_bias_ref,
    routes_ref,
    bias_ref,
    down_bias_ref,
    small_sems,
    load_sems,
    send_sems,
    recv_sems,
):
    half_rows = rows // 2
    hidden = down.shape[0]
    span = 8 * rows
    tail = width // 128 * 128
    req, tp = lax.axis_index("req"), lax.axis_index("tp")
    expert = req // 2
    step_width = 384
    steps = [(start, min(step_width, width - start)) for start in range(0, width, step_width)]
    links = {
        "x": (0, 1),
        "y": (2, 0),
        "c": (1, 0),
        "z1": (4, 0),
        "z2": (8, 0),
        "z3": (12, 0),
    }
    peers = {link: peer(*way) for link, way in links.items()}

    small = [
        pltpu.make_async_copy(source, target, small_sems.at[number])
        for number, (source, target) in enumerate(
            (
                (attn_hbm, attn_ref),
                (residual_hbm, residual_ref),
                (o_bias_hbm, o_bias_ref),
                (post_gain_hbm, post_gain_ref),
                (next_gain_hbm, next_gain_ref),
                (router_hbm, router_ref),
                (router_bias_hbm, router_bias_ref),
                (routes_hbm, routes_ref),
                (bias_hbm, bias_ref),
                (down_bias_hbm, down_bias_ref),
            )
        )
    ]
    small[0].start()
    loads = []
    for number, (start, size) in enumerate(steps):
        here = pl.ds(start, size)
        loads.append(
            pltpu.make_async_copy(o_weight_ref.at[here, :], o_weight.at[here, :], load_sems.at[number])
        )
    loads.append(pltpu.make_async_copy(gate_up_ref, gate_up, load_sems.at[len(steps)]))
    loads.append(pltpu.make_async_copy(down_ref, down, load_sems.at[len(steps) + 1]))
    for load in loads[:2] + small[1:] + loads[2:]:
        load.start()
    barrier = pltpu.get_barrier_semaphore()
    for link in peers:
        pl.semaphore_signal(
            barrier, inc=1, device_id=peers[link], device_id_type=pl.DeviceIdType.MESH
        )

    copies = {}

    def send(name, link, source, target):
        number = len(copies)
        copies[name] = pltpu.make_async_remote_copy(
            src_ref=source,
            dst_ref=target,
            send_sem=send_sems.at[number],
            recv_sem=recv_sems.at[number],
            device_id=peers[link],
            device_id_type=pl.DeviceIdType.MESH,
        )
        copies[name].start()

    def arrived(name):
        copies[name].wait_recv()

    def place(layer, core, spot, half=0):
        return ((layer * 2 + core) * 4 + spot) * rows + half * half_rows

    def block(ref, layer, core, spot):
        return ref.at[pl.ds(place(layer, core, spot), rows), :]

    def piece(ref, layer, core, spot, half):
        return ref.at[pl.ds(place(layer, core, spot, half), half_rows), :]

    small[0].wait()
    attn[0:rows, :] = attn_ref[pl.ds(pl.multiple_of(tp * rows, rows), rows), :]
    attn[rows:, :] = attn_ref[pl.ds(pl.multiple_of((1 - tp) * rows, rows), rows), :]
    for number, (start, size) in enumerate(steps):
        loads[number].wait()
        both = lax.dot_general(
            attn[...],
            o_weight[start : start + size, :],
            (((1,), (1,)), ((), ())),
            preferred_element_type=jnp.float32,
        )
        proj[:, start : start + size] = both[0:rows]
        proj_out[:, start : start + size] = both[rows:].astype(jnp.bfloat16)
        if number == 0:
            pl.semaphore_wait(barrier, len(links))
        here = pl.ds(start, size)
        send(("proj", number), "x", proj_out.at[:, here], proj_in.at[:, here])

    def op_pre():
        for load in small[1:]:
            load.wait()
        for number, ref in enumerate((o_bias_ref, post_gain_ref, next_gain_ref)):
            vectors_ref[number : number + 1, :] = ref[...].astype(jnp.float32).reshape(1, width)
        squares = jnp.zeros((rows, 1), jnp.float32)
        for number, (start, size) in enumerate(steps):
            here = slice(start, start + size)
            arrived(("proj", number))
            state = (
                residual_ref[:, here].astype(jnp.float32)
                + (proj[:, here] + proj_in[:, here].astype(jnp.float32))
                + vectors_ref[0:1, here]
            ).astype(jnp.bfloat16).astype(jnp.float32)
            base[:, here] = state
            squares = squares + jnp.sum(state * state, axis=1, keepdims=True)
        scale = lax.rsqrt(squares / width + 1e-05)
        padded_rows[:, tail:] = jnp.zeros((rows, padded_rows.shape[1] - tail), jnp.float32)
        padded_rows[:, 0:width] = base[...] * scale * vectors_ref[1:2, :]
        normed = padded_rows[:, 0:width].astype(jnp.bfloat16)
        logits = (
            lax.dot_general(
                normed,
                router_ref[...],
                (((1,), (1,)), ((), ())),
                preferred_element_type=jnp.float32,
            )
            + router_bias_ref[...]
        )
        given = routes_ref[...].astype(jnp.float32)
        here = (rows, given.shape[1])
        mine = lax.broadcasted_iota(jnp.int32, here, 0) + tp * rows
        mine = (mine == lax.broadcasted_iota(jnp.int32, here, 1)).astype(jnp.float32)
        routes = lax.dot_general(
            mine, given, (((1,), (1,)), ((), ())), preferred_element_type=jnp.float32
        )
        lane = lax.broadcasted_iota(jnp.int32, logits.shape, 1).astype(jnp.float32)
        hit = lane == routes[:, 0:1]
        for number in range(1, routes.shape[1]):
            hit = hit | (lane == routes[:, number : number + 1])
        expo = jnp.where(hit, jnp.exp(logits), 0.0)
        table = expo / jnp.sum(expo, axis=1, keepdims=True)
        high = table.astype(jnp.bfloat16).astype(jnp.float32)
        low = (table - high).astype(jnp.bfloat16).astype(jnp.float32)
        last = padded_rows[:, tail:]
        lane = lax.broadcasted_iota(jnp.int32, last.shape, 1) - (width - tail)
        for number in range(experts):
            last = jnp.where(lane == number, high[:, number : number + 1], last)
            last = jnp.where(lane == number + experts, low[:, number : number + 1], last)
        gathered[0:rows, 0:tail] = padded_rows[:, 0:tail].astype(jnp.bfloat16)
        gathered[0:rows, tail:] = last.astype(jnp.bfloat16)
        padded_rows[:, tail:] = last

    def op_bias():
        last = padded_rows[:, tail:]
        lane = lax.broadcasted_iota(jnp.int32, last.shape, 1) - (width - tail)
        for start, size in steps:
            here = slice(start, start + size)
            total = base[:, here]
            for number in range(experts):
                mine = (lane == number) | (lane == number + experts)
                weight = jnp.sum(jnp.where(mine, last, 0.0), axis=1, keepdims=True)
                total = total + weight * down_bias_ref[number : number + 1, here].astype(jnp.float32)
            base[:, here] = total

    def across(layer, spot):
        send(
            ("c", layer, spot),
            "c",
            block(gathered, layer, 0, spot),
            block(gathered, layer, 1, spot),
        )

    def along(name, link, layer, spot, half, far_layer, far_spot):
        send(
            name, link, piece(gathered, layer, 0, spot, half), piece(gathered, far_layer, 0, far_spot, half)
        )

    def spread(layer):
        if layer in GATHER_WIDE:
            along(("x", layer), "x", layer, 0, 1, layer, 1)
            along(("y", layer), "y", layer, 0, 0, layer, 2)
        else:
            own = block(gathered, layer, 0, 0)
            send(("x", layer), "x", own, block(gathered, layer, 0, 1))
            send(("y", layer), "y", own, block(gathered, layer, 0, 2))
        across(layer, 0)

    def op_own():
        spread(0)

    def op_own2():
        send("z2", "z2", block(gathered, 0, 0, 0), block(gathered, 2, 0, 0))

    def op_own1():
        send("z1", "z1", block(gathered, 0, 0, 0), block(gathered, 1, 0, 0))

    def op_z1():
        arrived("z1")

    def op_z2():
        arrived("z2")
        send("z3", "z1", block(gathered, 2, 0, 0), block(gathered, 3, 0, 0))

    def op_z3():
        arrived("z3")

    def op_rx(layer):
        arrived(("x", layer))
        if layer not in GATHER_WIDE:
            along(("yd", layer), "y", layer, 1, 1, layer, 3)
            across(layer, 1)

    def op_ry(layer):
        arrived(("y", layer))
        if layer not in GATHER_WIDE:
            along(("xd", layer), "x", layer, 2, 0, layer, 3)
            across(layer, 2)

    def op_wz(layer):
        source = 2 if layer == 3 else 0
        link = "z1" if layer == 3 else "z" + str(layer)
        along(("zx", layer), link, source, 1, 0, layer, 1)
        along(("zy", layer), link, source, 2, 1, layer, 2)

    def op_wd(layer):
        arrived(("zx", layer))
        along(("yd", layer), "y", layer, 1, 0, layer, 3)
        arrived(("zy", layer))
        along(("xd", layer), "x", layer, 2, 1, layer, 3)

    def op_wc(layer):
        across(layer, 1)
        across(layer, 2)

    def op_rd(layer):
        arrived(("xd", layer))
        arrived(("yd", layer))
        across(layer, 3)

    def op_dd(layer):
        for spot in range(4):
            arrived(("c", layer, spot))

    def op_w(number):
        loads[len(steps) + number].wait()

    def op_up(layer, step):
        here = pl.ds(layer * span, span)
        start = step * 256
        size = min(256, hidden - start)
        sides = []
        for side in range(2):
            sides.append(
                lax.dot_general(
                    gathered[here, 0:width],
                    gate_up[pl.ds(side * hidden + start, size), :],
                    (((1,), (1,)), ((), ())),
                    preferred_element_type=jnp.float32,
                )
                + bias_ref[side : side + 1, start : start + size].astype(jnp.float32)
            )
        gate = jnp.minimum(sides[0], 7.0)
        upper = jnp.clip(sides[1], -7.0, 7.0)
        act[:, start : start + size] = (
            (upper + 1.0) * gate * jax.nn.sigmoid(1.702 * gate)
        ).astype(jnp.bfloat16)

    def op_dn(layer, step):
        here = pl.ds(layer * span, span)
        extra = gathered[here, tail:].astype(jnp.float32)
        lane = lax.broadcasted_iota(jnp.int32, extra.shape, 1) - (width - tail)
        mine = (lane == expert) | (lane == expert + experts)
        share = jnp.sum(jnp.where(mine, extra, 0.0), axis=1, keepdims=True)
        start = step * 768
        size = min(768, width - start)
        partial[here, start : start + size] = (
            jnp.dot(act[...], down[:, start : start + size], preferred_element_type=jnp.float32)
            * share
        ).astype(jnp.bfloat16)

    cut = width // 256 // 2 * 256 + 256
    columns = ((0, cut), (cut, width - cut))

    def op_cs(layer, part):
        here = pl.ds(*columns[part])
        send(
            ("cs", layer, part),
            "c",
            partial.at[pl.ds(place(layer, 1, 0), 4 * rows), here],
            core_in.at[pl.ds(layer * 4 * rows, 4 * rows), here],
        )

    def add(part, start, size, *others):
        left, right = columns[part][0], sum(columns[part])
        total = partial[start : start + size, left:right].astype(jnp.float32)
        for other, first in others:
            total = total + other[first : first + size, left:right].astype(jnp.float32)
        partial[start : start + size, left:right] = total.astype(jnp.bfloat16)

    def half_place(layer, side, turn):
        return ((layer * 2 + side) * 2 + turn) * half_rows

    def send_half(part, layer, side, spot, half, turn):
        here = pl.ds(*columns[part])
        send(
            ("xy"[side] + "h", layer, turn, part),
            "xy"[side],
            partial.at[pl.ds(place(layer, 0, spot, half), half_rows), here],
            half_in.at[pl.ds(half_place(layer, side, turn), half_rows), here],
        )

    def add_half(part, layer, side, spot, half, turn):
        arrived(("xy"[side] + "h", layer, turn, part))
        add(part, place(layer, 0, spot, half), half_rows, (half_in, half_place(layer, side, turn)))

    def op_ca(layer, part):
        arrived(("cs", layer, part))
        first = layer * 4 * rows
        wide = layer in SUM_WIDE
        add(part, place(layer, 0, 3), rows, (core_in, first + 3 * rows))
        if wide:
            send_half(part, layer, 0, 3, 1, 0)
            send_half(part, layer, 1, 3, 0, 0)
        else:
            send_half(part, layer, 0, 3, 0, 0)
            send_half(part, layer, 1, 3, 1, 0)
        for spot in (1, 2):
            add(part, place(layer, 0, spot), rows, (core_in, first + spot * rows))
            if wide:
                send_half(part, layer, spot - 1, spot, 2 - spot, 1)
        add(part, place(layer, 0, 0), rows, (core_in, first))

    def op_ha(layer, part):
        here = pl.ds(*columns[part])
        if layer in SUM_WIDE:
            add_half(part, layer, 0, 2, 1, 0)
            add_half(part, layer, 1, 1, 0, 0)
            add_half(part, layer, 0, 0, 1, 1)
            add_half(part, layer, 1, 0, 0, 1)
            for turn, (spot, half, size) in enumerate(((1, 0, 1), (2, 1, 1), (0, 0, 2))):
                target = (layer * 2 - 2) * rows + turn * half_rows
                send(
                    ("zs", layer, turn, part),
                    "z" + str(layer),
                    partial.at[pl.ds(place(layer, 0, spot, half), size * half_rows), here],
                    layer_in.at[pl.ds(target, size * half_rows), here],
                )
            return
        add_half(part, layer, 0, 2, 0, 0)
        add_half(part, layer, 1, 1, 1, 0)
        for side, link in enumerate("xy"):
            send(
                (link + "f", layer, part),
                link,
                partial.at[pl.ds(place(layer, 0, 1 + side), rows), here],
                full_in.at[pl.ds((layer * 2 + side) * rows, rows), here],
            )

    def op_fa(layer, part):
        here = pl.ds(*columns[part])
        first = layer * 2 * rows
        arrived(("xf", layer, part))
        arrived(("yf", layer, part))
        add(part, place(layer, 0, 0), rows, (full_in, first), (full_in, first + rows))
        send(
            ("zs", layer, 2, part),
            "z" + str(layer),
            partial.at[pl.ds(place(layer, 0, 0), rows), here],
            layer_in.at[pl.ds((layer * 2 - 1) * rows, rows), here],
        )

    def op_za(layer, part):
        first = (layer * 2 - 2) * rows
        arrived(("zs", layer, 0, part))
        add(part, place(0, 0, 1, 0), half_rows, (layer_in, first))
        arrived(("zs", layer, 1, part))
        add(part, place(0, 0, 2, 1), half_rows, (layer_in, first + half_rows))

    def op_zt(layer, part):
        left, right = columns[part][0], sum(columns[part])
        first = (layer * 2 - 1) * rows
        arrived(("zs", layer, 2, part))
        base[:, left:right] += layer_in[first : first + rows, left:right].astype(jnp.float32)

    def op_fin():
        base[...] += partial[0:rows, :].astype(jnp.float32)
        squares = jnp.zeros((rows, 1), jnp.float32)
        for part, (left, size) in enumerate(columns):
            here = slice(left, left + size)
            arrived(("xf", 0, part))
            arrived(("yf", 0, part))
            total = base[:, here]
            for first in (0, rows):
                total = total + full_in[first : first + rows, here].astype(jnp.float32)
            total = total.astype(jnp.bfloat16).astype(jnp.float32)
            out_ref[0:rows, here] = total
            squares = squares + jnp.sum(total * total, axis=1, keepdims=True)
        scale = lax.rsqrt(squares / width + 1e-05)
        out_ref[rows:, :] = out_ref[0:rows, :] * scale * vectors_ref[2:3, :]

    ops = dict(
        pre=op_pre, bias=op_bias, own=op_own, ownb=op_own2, ownc=op_own1, w=op_w, z1=op_z1, z2=op_z2, z3=op_z3,
        s=spread, rx=op_rx, ry=op_ry, wz=op_wz, wd=op_wd, wc=op_wc, rd=op_rd, dd=op_dd, up=op_up,
        dn=op_dn, cs=op_cs, ca=op_ca, ha=op_ha, fa=op_fa, za=op_za, zt=op_zt, fin=op_fin,
    )
    for name in PLAN:
        if name in ops:
            ops[name]()
        else:
            stem = name.rstrip("0123456789")
            ops[stem](*[int(digit) for digit in name[len(stem) :]])
    for copy in copies.values():
        copy.wait_send()


def whole_layer(
    attn_ctx,
    o_weight,
    o_bias,
    residual,
    post_gain,
    router_weight,
    router_bias,
    routes,
    gate_up_weight,
    gate_up_bias,
    down_weight,
    down_bias,
    next_gain,
):
    rows, width = residual.shape
    experts = router_bias.shape[0]
    hidden = down_weight.shape[1]
    padded = (width + 2 * experts + 127) // 128 * 128
    gate_up = jnp.transpose(gate_up_weight[0], (1, 2, 0)).reshape(2 * hidden, width)
    bias = gate_up_bias[0]
    vmem = pl.BlockSpec(memory_space=pltpu.VMEM)
    hbm = pl.BlockSpec(memory_space=pl.ANY)
    copies = 160
    out = pl.pallas_call(
        functools.partial(layer_kernel, rows, width, experts),
        out_shape=jax.ShapeDtypeStruct((2 * rows, width), jnp.float32),
        in_specs=[hbm] * 13,
        out_specs=vmem,
        scratch_shapes=[
            pltpu.VMEM((32 * rows, padded), jnp.bfloat16),
            pltpu.VMEM((32 * rows, width), jnp.bfloat16),
            pltpu.VMEM((16 * rows, width), jnp.bfloat16),
            pltpu.VMEM((8 * rows, width), jnp.bfloat16),
            pltpu.VMEM((8 * rows, width), jnp.bfloat16),
            pltpu.VMEM((6 * rows, width), jnp.bfloat16),
            pltpu.VMEM((width, attn_ctx.shape[1]), jnp.bfloat16),
            pltpu.VMEM((2 * hidden, width), jnp.bfloat16),
            pltpu.VMEM((hidden, width), jnp.bfloat16),
            pltpu.VMEM((8 * rows, hidden), jnp.bfloat16),
            pltpu.VMEM(attn_ctx.shape, jnp.bfloat16),
            pltpu.VMEM((rows, width), jnp.float32),
            pltpu.VMEM((rows, width), jnp.bfloat16),
            pltpu.VMEM((rows, width), jnp.bfloat16),
            pltpu.VMEM((rows, padded), jnp.float32),
            pltpu.VMEM((rows, width), jnp.float32),
            pltpu.VMEM(attn_ctx.shape, jnp.bfloat16),
            pltpu.VMEM((rows, width), jnp.bfloat16),
            pltpu.VMEM((width,), jnp.bfloat16),
            pltpu.VMEM((width,), jnp.bfloat16),
            pltpu.VMEM((width,), jnp.bfloat16),
            pltpu.VMEM((3, width), jnp.float32),
            pltpu.VMEM((experts, width), jnp.bfloat16),
            pltpu.VMEM((1, experts), jnp.float32),
            pltpu.VMEM(routes.shape[::-1], jnp.int32),
            pltpu.VMEM((2, hidden), jnp.bfloat16),
            pltpu.VMEM((experts, width), jnp.bfloat16),
            pltpu.SemaphoreType.DMA((10,)),
            pltpu.SemaphoreType.DMA((16,)),
            pltpu.SemaphoreType.DMA((copies,)),
            pltpu.SemaphoreType.DMA((copies,)),
        ],
        compiler_params=pltpu.CompilerParams(
            collective_id=0, has_side_effects=True, vmem_limit_bytes=59392 * 1024
        ),
    )(
        attn_ctx,
        o_weight.T,
        residual,
        o_bias,
        post_gain,
        next_gain,
        router_weight.T,
        router_bias.reshape(1, experts),
        routes.T,
        gate_up,
        bias,
        down_weight[0],
        down_bias,
    )
    return (out[:rows].astype(jnp.bfloat16), out[rows:].astype(jnp.bfloat16))


def per_device(
    attn_ctx,
    o_weight,
    o_bias,
    residual,
    post_gain,
    router_weight,
    router_bias,
    routes,
    gate_up_weight,
    gate_up_bias,
    down_weight,
    down_bias,
    next_gain,
):
    req_count = lax.axis_size("req")
    tp_count = lax.axis_size("tp")
    width = o_weight.shape[1]
    tokens_here = attn_ctx.shape[0]
    own_rows = tokens_here // tp_count
    experts = req_count // 2
    top_count = routes.shape[1]
    capacity = min(own_rows, max(2, 2 * top_count * own_rows // experts))
    if capacity == own_rows and req_count == 16 and tp_count == 2 and own_rows % 32 == 0:
        return whole_layer(
            attn_ctx,
            o_weight,
            o_bias,
            residual,
            post_gain,
            router_weight,
            router_bias,
            routes,
            gate_up_weight,
            gate_up_bias,
            down_weight,
            down_bias,
            next_gain,
        )
    own_start = lax.axis_index("tp") * own_rows
    bias_vec = o_bias.astype(jnp.float32)
    proj = jnp.dot(attn_ctx, o_weight, preferred_element_type=jnp.float32).astype(jnp.bfloat16)
    if tp_count == 2:
        theirs = lax.dynamic_slice_in_dim(proj, own_rows - own_start, own_rows, 0)
        mine = lax.dynamic_slice_in_dim(proj, own_start, own_rows, 0)
        arrived = lax.ppermute(theirs, "tp", [(0, 1), (1, 0)])
        summed = mine.astype(jnp.float32) + arrived.astype(jnp.float32)
    else:
        summed = lax.psum_scatter(proj, "tp", scatter_dimension=0, tiled=True).astype(jnp.float32)
    state = (residual.astype(jnp.float32) + summed + bias_vec).astype(jnp.bfloat16)
    own_routes = lax.dynamic_slice_in_dim(routes, own_start, own_rows, 0)
    normed, weights, table = route_rows(
        state, own_routes, post_gain, router_weight, router_bias, experts
    )
    bias_terms = jnp.dot(table, down_bias.astype(jnp.float32), precision=lax.Precision.HIGHEST)
    slots = slot_numbers(own_routes.reshape(1, own_rows * top_count), experts, capacity)
    targets = 2 * own_routes.reshape(-1) * capacity + slots.reshape(-1)
    outgoing = place_rows(normed, targets, capacity, req_count, top_count)
    incoming = lax.all_to_all(outgoing, "req", split_axis=0, concat_axis=0, tiled=True)
    gathered = lax.all_gather(incoming[None], "tp", axis=0, tiled=True).reshape(-1, width)
    sums = lax.psum_scatter(
        expert_apply(gathered, gate_up_weight, gate_up_bias, down_weight).astype(jnp.bfloat16),
        "tp",
        scatter_dimension=0,
        tiled=True,
    ).astype(jnp.float32)
    returned = lax.all_to_all(
        sums.reshape(req_count, capacity, width).astype(jnp.bfloat16),
        "req",
        split_axis=0,
        concat_axis=0,
        tiled=True,
    ).astype(jnp.float32)
    mixed = weigh_parts(returned.reshape(-1, width), targets, capacity, weights, top_count)
    hidden_state = (state.astype(jnp.float32) + mixed + bias_terms).astype(jnp.bfloat16)
    normed_out = rms_norm(hidden_state.astype(jnp.float32), next_gain).astype(jnp.bfloat16)
    return (hidden_state, normed_out)


def solution(mesh):
    return jax.shard_map(
        per_device,
        mesh=mesh,
        in_specs=(
            P("req", "tp"),
            P("tp", None),
            P(),
            P(("req", "tp"), None),
            P(),
            P(),
            P(),
            P("req", None),
            P("req", None, None, "tp"),
            P("req", None, "tp"),
            P("req", "tp", None),
            P(),
            P(),
        ),
        out_specs=(P(("req", "tp"), None), P(("req", "tp"), None)),
        check_vma=False,
    )
```

```python
import functools

import jax
import jax.numpy as jnp
from jax import lax
from jax.experimental import pallas as pl
from jax.experimental.pallas import tpu as pltpu
from jax.sharding import PartitionSpec as P


def rms_norm(values, gain):
    scale = lax.rsqrt(jnp.mean(values * values, axis=-1, keepdims=True) + 1e-05)
    return values * scale * gain.astype(jnp.float32)


def route_rows(state, route_ids, post_gain, router_weight, router_bias, experts):
    normed = rms_norm(state.astype(jnp.float32), post_gain).astype(jnp.bfloat16)
    logits = jnp.dot(normed, router_weight, preferred_element_type=jnp.float32) + router_bias
    onehot = (route_ids[:, :, None] == jnp.arange(experts, dtype=jnp.int32)[None, None, :]).astype(
        jnp.float32
    )
    picked = jnp.sum(onehot * logits[:, None, :], axis=2)
    expo = jnp.exp(picked)
    weights = expo / jnp.sum(expo, axis=1, keepdims=True)
    table = jnp.sum(onehot * weights[:, :, None], axis=1)
    return (normed, weights, table)


def slot_numbers(route_blocks, experts, capacity):
    onehot = (
        route_blocks[:, :, None] == jnp.arange(experts, dtype=jnp.int32)[None, None, :]
    ).astype(jnp.int32)
    earlier = jnp.tril(jnp.ones((onehot.shape[1],) * 2, jnp.float32), -1)
    ranks = jnp.einsum("pq,bqe->bpe", earlier, onehot.astype(jnp.float32)).astype(jnp.int32)
    slots = jnp.sum(ranks * onehot, axis=2)
    offsets = jnp.arange(route_blocks.shape[0], dtype=jnp.int32)[:, None] * capacity
    return slots + offsets


def place_rows(normed, targets, block, req_count, top_count):
    width = normed.shape[1]
    source = jnp.repeat(normed, top_count, axis=0)
    buffer = jnp.zeros((req_count * block, width), jnp.bfloat16)
    index = jnp.concatenate([targets, targets + block])
    buffer = buffer.at[index].set(jnp.concatenate([source, source], axis=0))
    return buffer.reshape(req_count, block, width)


def weigh_parts(flat, targets, block, weights, top_count):
    first = jnp.take(flat, targets, axis=0).astype(jnp.float32)
    second = jnp.take(flat, targets + block, axis=0).astype(jnp.float32)
    values = (first + second) * weights.reshape(-1)[:, None]
    return jnp.sum(values.reshape(-1, top_count, flat.shape[1]), axis=1)


def expert_apply(rows, gate_up_weight, gate_up_bias, down_weight):
    local_width = gate_up_weight.shape[3]
    weight_mat = gate_up_weight[0].reshape(gate_up_weight.shape[1], 2 * local_width)
    projected = jnp.dot(rows, weight_mat, preferred_element_type=jnp.float32)
    projected = projected + gate_up_bias[0].reshape(2 * local_width).astype(jnp.float32)
    gate = jnp.minimum(projected[:, :local_width], 7.0)
    upper = jnp.clip(projected[:, local_width:], -7.0, 7.0)
    act = ((upper + 1.0) * gate * jax.nn.sigmoid(1.702 * gate)).astype(jnp.bfloat16)
    return jnp.dot(act, down_weight[0], preferred_element_type=jnp.float32)


def peer(bits, stride_x):
    req, tp = lax.axis_index("req"), lax.axis_index("tp")
    for bit in (1, 2, 4, 8):
        if bits & bit:
            req = req + bit * (1 - 2 * ((req // bit) % 2))
    return {"req": req, "tp": 1 - tp if stride_x else tp}


GATHER_WIDE = (1,)
SUM_WIDE = (1,)
PLAN = (
    "pre", "own", "ownc", "bias", "ownb", "rx0", "ry0", "wz1", "z1", "s1", "rd0", "z2", "dd0",
    "s2", "w0", "up00", "rx1", "up01", "wd1", "ry1", "up02", "w1", "dn00", "wc1", "dn01",
    "rx2", "ry2", "dn02", "cs00", "z3", "dn03", "rd1", "s3", "ca00", "dd1", "up10", "up11",
    "up12", "rd2", "dn10", "dn11", "dn12", "dn13", "rx3", "dd2", "ry3", "cs10", "cs11", "up20",
    "up21", "ca10", "up22", "dn20", "rd3", "dn21", "dn22", "cs20", "ca11", "dd3", "dn23",
    "cs21", "up30", "ca20", "ha10", "ca21", "up31", "ha20", "up32", "dn30", "ha21", "dn31",
    "cs01", "ha11", "cs30", "za10", "dn32", "dn33", "fa20", "ca30", "ha30", "fa21", "cs31",
    "za11", "ca31", "ca01", "zt11", "fa30", "ha31", "ha00", "zt10", "fa31", "zt30", "zt20",
    "zt21", "ha01", "zt31", "fin",
)


def layer_kernel(
    rows,
    width,
    experts,
    attn_hbm,
    o_weight_ref,
    residual_hbm,
    o_bias_hbm,
    post_gain_hbm,
    next_gain_hbm,
    router_hbm,
    router_bias_hbm,
    routes_hbm,
    gate_up_ref,
    bias_hbm,
    down_ref,
    down_bias_hbm,
    out_ref,
    gathered,
    partial,
    core_in,
    half_in,
    full_in,
    layer_in,
    o_weight,
    gate_up,
    down,
    act,
    attn,
    proj,
    proj_out,
    proj_in,
    padded_rows,
    base,
    attn_ref,
    residual_ref,
    o_bias_ref,
    post_gain_ref,
    next_gain_ref,
    vectors_ref,
    router_ref,
    router_bias_ref,
    routes_ref,
    bias_ref,
    down_bias_ref,
    small_sems,
    load_sems,
    send_sems,
    recv_sems,
):
    half_rows = rows // 2
    hidden = down.shape[0]
    span = 8 * rows
    tail = width // 128 * 128
    req, tp = lax.axis_index("req"), lax.axis_index("tp")
    expert = req // 2
    step_width = 384
    steps = [(start, min(step_width, width - start)) for start in range(0, width, step_width)]
    links = {
        "x": (0, 1),
        "y": (2, 0),
        "c": (1, 0),
        "z1": (4, 0),
        "z2": (8, 0),
        "z3": (12, 0),
    }
    peers = {link: peer(*way) for link, way in links.items()}

    small = [
        pltpu.make_async_copy(source, target, small_sems.at[number])
        for number, (source, target) in enumerate(
            (
                (attn_hbm, attn_ref),
                (residual_hbm, residual_ref),
                (o_bias_hbm, o_bias_ref),
                (post_gain_hbm, post_gain_ref),
                (next_gain_hbm, next_gain_ref),
                (router_hbm, router_ref),
                (router_bias_hbm, router_bias_ref),
                (routes_hbm, routes_ref),
                (bias_hbm, bias_ref),
                (down_bias_hbm, down_bias_ref),
            )
        )
    ]
    small[0].start()
    loads = []
    for number, (start, size) in enumerate(steps):
        here = pl.ds(start, size)
        loads.append(
            pltpu.make_async_copy(o_weight_ref.at[here, :], o_weight.at[here, :], load_sems.at[number])
        )
    loads.append(pltpu.make_async_copy(gate_up_ref, gate_up, load_sems.at[len(steps)]))
    loads.append(pltpu.make_async_copy(down_ref, down, load_sems.at[len(steps) + 1]))
    ahead = 3
    for load in loads[:1] + small[1:] + loads[1:ahead]:
        load.start()
    barrier = pltpu.get_barrier_semaphore()
    for link in peers:
        pl.semaphore_signal(
            barrier, inc=1, device_id=peers[link], device_id_type=pl.DeviceIdType.MESH
        )

    copies = {}

    def send(name, link, source, target):
        number = len(copies)
        copies[name] = pltpu.make_async_remote_copy(
            src_ref=source,
            dst_ref=target,
            send_sem=send_sems.at[number],
            recv_sem=recv_sems.at[number],
            device_id=peers[link],
            device_id_type=pl.DeviceIdType.MESH,
        )
        copies[name].start()

    def arrived(name):
        copies[name].wait_recv()

    def place(layer, core, spot, half=0):
        return ((layer * 2 + core) * 4 + spot) * rows + half * half_rows

    def block(ref, layer, core, spot):
        return ref.at[pl.ds(place(layer, core, spot), rows), :]

    def piece(ref, layer, core, spot, half):
        return ref.at[pl.ds(place(layer, core, spot, half), half_rows), :]

    small[0].wait()
    attn[0:rows, :] = attn_ref[pl.ds(pl.multiple_of(tp * rows, rows), rows), :]
    attn[rows:, :] = attn_ref[pl.ds(pl.multiple_of((1 - tp) * rows, rows), rows), :]
    for number, (start, size) in enumerate(steps):
        loads[number].wait()
        for load in loads[number + ahead : number + ahead + 1]:
            load.start()
        both = lax.dot_general(
            attn[...],
            o_weight[start : start + size, :],
            (((1,), (1,)), ((), ())),
            preferred_element_type=jnp.float32,
        )
        proj[:, start : start + size] = both[0:rows]
        proj_out[:, start : start + size] = both[rows:].astype(jnp.bfloat16)
        if number == 0:
            pl.semaphore_wait(barrier, len(links))
        here = pl.ds(start, size)
        send(("proj", number), "x", proj_out.at[:, here], proj_in.at[:, here])

    def op_pre():
        for load in small[1:]:
            load.wait()
        for number, ref in enumerate((o_bias_ref, post_gain_ref, next_gain_ref)):
            vectors_ref[number : number + 1, :] = ref[...].astype(jnp.float32).reshape(1, width)
        squares = jnp.zeros((rows, 1), jnp.float32)
        for number, (start, size) in enumerate(steps):
            here = slice(start, start + size)
            arrived(("proj", number))
            state = (
                residual_ref[:, here].astype(jnp.float32)
                + (proj[:, here] + proj_in[:, here].astype(jnp.float32))
                + vectors_ref[0:1, here]
            ).astype(jnp.bfloat16).astype(jnp.float32)
            base[:, here] = state
            squares = squares + jnp.sum(state * state, axis=1, keepdims=True)
        scale = lax.rsqrt(squares / width + 1e-05)
        padded_rows[:, tail:] = jnp.zeros((rows, padded_rows.shape[1] - tail), jnp.float32)
        padded_rows[:, 0:width] = base[...] * scale * vectors_ref[1:2, :]
        normed = padded_rows[:, 0:width].astype(jnp.bfloat16)
        logits = (
            lax.dot_general(
                normed,
                router_ref[...],
                (((1,), (1,)), ((), ())),
                preferred_element_type=jnp.float32,
            )
            + router_bias_ref[...]
        )
        given = routes_ref[...].astype(jnp.float32)
        here = (rows, given.shape[1])
        mine = lax.broadcasted_iota(jnp.int32, here, 0) + tp * rows
        mine = (mine == lax.broadcasted_iota(jnp.int32, here, 1)).astype(jnp.float32)
        routes = lax.dot_general(
            mine, given, (((1,), (1,)), ((), ())), preferred_element_type=jnp.float32
        )
        lane = lax.broadcasted_iota(jnp.int32, logits.shape, 1).astype(jnp.float32)
        hit = lane == routes[:, 0:1]
        for number in range(1, routes.shape[1]):
            hit = hit | (lane == routes[:, number : number + 1])
        expo = jnp.where(hit, jnp.exp(logits), 0.0)
        table = expo / jnp.sum(expo, axis=1, keepdims=True)
        high = table.astype(jnp.bfloat16).astype(jnp.float32)
        low = (table - high).astype(jnp.bfloat16).astype(jnp.float32)
        last = padded_rows[:, tail:]
        lane = lax.broadcasted_iota(jnp.int32, last.shape, 1) - (width - tail)
        for number in range(experts):
            last = jnp.where(lane == number, high[:, number : number + 1], last)
            last = jnp.where(lane == number + experts, low[:, number : number + 1], last)
        gathered[0:rows, 0:tail] = padded_rows[:, 0:tail].astype(jnp.bfloat16)
        gathered[0:rows, tail:] = last.astype(jnp.bfloat16)
        padded_rows[:, tail:] = last

    def op_bias():
        last = padded_rows[:, tail:]
        lane = lax.broadcasted_iota(jnp.int32, last.shape, 1) - (width - tail)
        for start, size in steps:
            here = slice(start, start + size)
            total = base[:, here]
            for number in range(experts):
                mine = (lane == number) | (lane == number + experts)
                weight = jnp.sum(jnp.where(mine, last, 0.0), axis=1, keepdims=True)
                total = total + weight * down_bias_ref[number : number + 1, here].astype(jnp.float32)
            base[:, here] = total

    def across(layer, spot):
        send(
            ("c", layer, spot),
            "c",
            block(gathered, layer, 0, spot),
            block(gathered, layer, 1, spot),
        )

    def along(name, link, layer, spot, half, far_layer, far_spot):
        send(
            name, link, piece(gathered, layer, 0, spot, half), piece(gathered, far_layer, 0, far_spot, half)
        )

    def spread(layer):
        if layer in GATHER_WIDE:
            along(("x", layer), "x", layer, 0, 1, layer, 1)
            along(("y", layer), "y", layer, 0, 0, layer, 2)
        else:
            own = block(gathered, layer, 0, 0)
            send(("x", layer), "x", own, block(gathered, layer, 0, 1))
            send(("y", layer), "y", own, block(gathered, layer, 0, 2))
        across(layer, 0)

    def op_own():
        spread(0)

    def op_own2():
        send("z2", "z2", block(gathered, 0, 0, 0), block(gathered, 2, 0, 0))

    def op_own1():
        send("z1", "z1", block(gathered, 0, 0, 0), block(gathered, 1, 0, 0))

    def op_z1():
        arrived("z1")

    def op_z2():
        arrived("z2")
        send("z3", "z1", block(gathered, 2, 0, 0), block(gathered, 3, 0, 0))

    def op_z3():
        arrived("z3")

    def op_rx(layer):
        arrived(("x", layer))
        if layer not in GATHER_WIDE:
            along(("yd", layer), "y", layer, 1, 1, layer, 3)
            across(layer, 1)

    def op_ry(layer):
        arrived(("y", layer))
        if layer not in GATHER_WIDE:
            along(("xd", layer), "x", layer, 2, 0, layer, 3)
            across(layer, 2)

    def op_wz(layer):
        source = 2 if layer == 3 else 0
        link = "z1" if layer == 3 else "z" + str(layer)
        along(("zx", layer), link, source, 1, 0, layer, 1)
        along(("zy", layer), link, source, 2, 1, layer, 2)

    def op_wd(layer):
        arrived(("zx", layer))
        along(("yd", layer), "y", layer, 1, 0, layer, 3)
        arrived(("zy", layer))
        along(("xd", layer), "x", layer, 2, 1, layer, 3)

    def op_wc(layer):
        across(layer, 1)
        across(layer, 2)

    def op_rd(layer):
        arrived(("xd", layer))
        arrived(("yd", layer))
        across(layer, 3)

    def op_dd(layer):
        for spot in range(4):
            arrived(("c", layer, spot))

    for load in loads[len(steps) + ahead :]:
        load.start()

    def op_w(number):
        loads[len(steps) + number].wait()

    def op_up(layer, step):
        here = pl.ds(layer * span, span)
        start = step * 256
        size = min(256, hidden - start)
        sides = []
        for side in range(2):
            sides.append(
                lax.dot_general(
                    gathered[here, 0:width],
                    gate_up[pl.ds(side * hidden + start, size), :],
                    (((1,), (1,)), ((), ())),
                    preferred_element_type=jnp.float32,
                )
                + bias_ref[side : side + 1, start : start + size].astype(jnp.float32)
            )
        gate = jnp.minimum(sides[0], 7.0)
        upper = jnp.clip(sides[1], -7.0, 7.0)
        act[:, start : start + size] = (
            (upper + 1.0) * gate * jax.nn.sigmoid(1.702 * gate)
        ).astype(jnp.bfloat16)

    def op_dn(layer, step):
        here = pl.ds(layer * span, span)
        extra = gathered[here, tail:].astype(jnp.float32)
        lane = lax.broadcasted_iota(jnp.int32, extra.shape, 1) - (width - tail)
        mine = (lane == expert) | (lane == expert + experts)
        share = jnp.sum(jnp.where(mine, extra, 0.0), axis=1, keepdims=True)
        start = step * 768
        size = min(768, width - start)
        partial[here, start : start + size] = (
            jnp.dot(act[...], down[:, start : start + size], preferred_element_type=jnp.float32)
            * share
        ).astype(jnp.bfloat16)

    cut = width // 256 // 2 * 256 + 256
    columns = ((0, cut), (cut, width - cut))

    def op_cs(layer, part):
        here = pl.ds(*columns[part])
        send(
            ("cs", layer, part),
            "c",
            partial.at[pl.ds(place(layer, 1, 0), 4 * rows), here],
            core_in.at[pl.ds(layer * 4 * rows, 4 * rows), here],
        )

    def add(part, start, size, *others):
        left, right = columns[part][0], sum(columns[part])
        if len(others) == 1:
            [(other, first)] = others
            partial[start : start + size, left:right] += other[first : first + size, left:right]
            return
        total = partial[start : start + size, left:right].astype(jnp.float32)
        for other, first in others:
            total = total + other[first : first + size, left:right].astype(jnp.float32)
        partial[start : start + size, left:right] = total.astype(jnp.bfloat16)

    def half_place(layer, side, turn):
        return ((layer * 2 + side) * 2 + turn) * half_rows

    def send_half(part, layer, side, spot, half, turn):
        here = pl.ds(*columns[part])
        send(
            ("xy"[side] + "h", layer, turn, part),
            "xy"[side],
            partial.at[pl.ds(place(layer, 0, spot, half), half_rows), here],
            half_in.at[pl.ds(half_place(layer, side, turn), half_rows), here],
        )

    def add_half(part, layer, side, spot, half, turn):
        arrived(("xy"[side] + "h", layer, turn, part))
        add(part, place(layer, 0, spot, half), half_rows, (half_in, half_place(layer, side, turn)))

    def op_ca(layer, part):
        arrived(("cs", layer, part))
        first = layer * 4 * rows
        wide = layer in SUM_WIDE
        add(part, place(layer, 0, 3), rows, (core_in, first + 3 * rows))
        if wide:
            send_half(part, layer, 0, 3, 1, 0)
            send_half(part, layer, 1, 3, 0, 0)
        else:
            send_half(part, layer, 0, 3, 0, 0)
            send_half(part, layer, 1, 3, 1, 0)
        for spot in (1, 2):
            add(part, place(layer, 0, spot), rows, (core_in, first + spot * rows))
            if wide:
                send_half(part, layer, spot - 1, spot, 2 - spot, 1)
        add(part, place(layer, 0, 0), rows, (core_in, first))

    def op_ha(layer, part):
        here = pl.ds(*columns[part])
        if layer in SUM_WIDE:
            add_half(part, layer, 0, 2, 1, 0)
            add_half(part, layer, 1, 1, 0, 0)
            add_half(part, layer, 0, 0, 1, 1)
            add_half(part, layer, 1, 0, 0, 1)
            for turn, (spot, half, size) in enumerate(((1, 0, 1), (2, 1, 1), (0, 0, 2))):
                target = (layer * 2 - 2) * rows + turn * half_rows
                send(
                    ("zs", layer, turn, part),
                    "z" + str(layer),
                    partial.at[pl.ds(place(layer, 0, spot, half), size * half_rows), here],
                    layer_in.at[pl.ds(target, size * half_rows), here],
                )
            return
        add_half(part, layer, 0, 2, 0, 0)
        add_half(part, layer, 1, 1, 1, 0)
        for side, link in enumerate("xy"):
            send(
                (link + "f", layer, part),
                link,
                partial.at[pl.ds(place(layer, 0, 1 + side), rows), here],
                full_in.at[pl.ds((layer * 2 + side) * rows, rows), here],
            )

    def op_fa(layer, part):
        here = pl.ds(*columns[part])
        first = layer * 2 * rows
        arrived(("xf", layer, part))
        arrived(("yf", layer, part))
        add(part, place(layer, 0, 0), rows, (full_in, first), (full_in, first + rows))
        send(
            ("zs", layer, 2, part),
            "z" + str(layer),
            partial.at[pl.ds(place(layer, 0, 0), rows), here],
            layer_in.at[pl.ds((layer * 2 - 1) * rows, rows), here],
        )

    def op_za(layer, part):
        first = (layer * 2 - 2) * rows
        arrived(("zs", layer, 0, part))
        add(part, place(0, 0, 1, 0), half_rows, (layer_in, first))
        arrived(("zs", layer, 1, part))
        add(part, place(0, 0, 2, 1), half_rows, (layer_in, first + half_rows))

    def op_zt(layer, part):
        left, right = columns[part][0], sum(columns[part])
        first = (layer * 2 - 1) * rows
        arrived(("zs", layer, 2, part))
        base[:, left:right] += layer_in[first : first + rows, left:right].astype(jnp.float32)

    def op_fin():
        base[...] += partial[0:rows, :].astype(jnp.float32)
        squares = jnp.zeros((rows, 1), jnp.float32)
        for part, (left, size) in enumerate(columns):
            here = slice(left, left + size)
            arrived(("xf", 0, part))
            arrived(("yf", 0, part))
            total = base[:, here]
            for first in (0, rows):
                total = total + full_in[first : first + rows, here].astype(jnp.float32)
            total = total.astype(jnp.bfloat16).astype(jnp.float32)
            out_ref[0:rows, here] = total
            squares = squares + jnp.sum(total * total, axis=1, keepdims=True)
        scale = lax.rsqrt(squares / width + 1e-05)
        out_ref[rows:, :] = out_ref[0:rows, :] * scale * vectors_ref[2:3, :]

    ops = dict(
        pre=op_pre, bias=op_bias, own=op_own, ownb=op_own2, ownc=op_own1, w=op_w, z1=op_z1, z2=op_z2, z3=op_z3,
        s=spread, rx=op_rx, ry=op_ry, wz=op_wz, wd=op_wd, wc=op_wc, rd=op_rd, dd=op_dd, up=op_up,
        dn=op_dn, cs=op_cs, ca=op_ca, ha=op_ha, fa=op_fa, za=op_za, zt=op_zt, fin=op_fin,
    )
    for name in PLAN:
        if name in ops:
            ops[name]()
        else:
            stem = name.rstrip("0123456789")
            ops[stem](*[int(digit) for digit in name[len(stem) :]])
    for copy in copies.values():
        copy.wait_send()


def whole_layer(
    attn_ctx,
    o_weight,
    o_bias,
    residual,
    post_gain,
    router_weight,
    router_bias,
    routes,
    gate_up_weight,
    gate_up_bias,
    down_weight,
    down_bias,
    next_gain,
):
    rows, width = residual.shape
    experts = router_bias.shape[0]
    hidden = down_weight.shape[1]
    padded = (width + 2 * experts + 127) // 128 * 128
    gate_up = jnp.transpose(gate_up_weight[0], (1, 2, 0)).reshape(2 * hidden, width)
    bias = gate_up_bias[0]
    vmem = pl.BlockSpec(memory_space=pltpu.VMEM)
    hbm = pl.BlockSpec(memory_space=pl.ANY)
    copies = 160
    out = pl.pallas_call(
        functools.partial(layer_kernel, rows, width, experts),
        out_shape=jax.ShapeDtypeStruct((2 * rows, width), jnp.float32),
        in_specs=[hbm] * 13,
        out_specs=vmem,
        scratch_shapes=[
            pltpu.VMEM((32 * rows, padded), jnp.bfloat16),
            pltpu.VMEM((32 * rows, width), jnp.bfloat16),
            pltpu.VMEM((16 * rows, width), jnp.bfloat16),
            pltpu.VMEM((8 * rows, width), jnp.bfloat16),
            pltpu.VMEM((8 * rows, width), jnp.bfloat16),
            pltpu.VMEM((6 * rows, width), jnp.bfloat16),
            pltpu.VMEM((width, attn_ctx.shape[1]), jnp.bfloat16),
            pltpu.VMEM((2 * hidden, width), jnp.bfloat16),
            pltpu.VMEM((hidden, width), jnp.bfloat16),
            pltpu.VMEM((8 * rows, hidden), jnp.bfloat16),
            pltpu.VMEM(attn_ctx.shape, jnp.bfloat16),
            pltpu.VMEM((rows, width), jnp.float32),
            pltpu.VMEM((rows, width), jnp.bfloat16),
            pltpu.VMEM((rows, width), jnp.bfloat16),
            pltpu.VMEM((rows, padded), jnp.float32),
            pltpu.VMEM((rows, width), jnp.float32),
            pltpu.VMEM(attn_ctx.shape, jnp.bfloat16),
            pltpu.VMEM((rows, width), jnp.bfloat16),
            pltpu.VMEM((width,), jnp.bfloat16),
            pltpu.VMEM((width,), jnp.bfloat16),
            pltpu.VMEM((width,), jnp.bfloat16),
            pltpu.VMEM((3, width), jnp.float32),
            pltpu.VMEM((experts, width), jnp.bfloat16),
            pltpu.VMEM((1, experts), jnp.float32),
            pltpu.VMEM(routes.shape[::-1], jnp.int32),
            pltpu.VMEM((2, hidden), jnp.bfloat16),
            pltpu.VMEM((experts, width), jnp.bfloat16),
            pltpu.SemaphoreType.DMA((10,)),
            pltpu.SemaphoreType.DMA((16,)),
            pltpu.SemaphoreType.DMA((copies,)),
            pltpu.SemaphoreType.DMA((copies,)),
        ],
        compiler_params=pltpu.CompilerParams(
            collective_id=0, has_side_effects=True, vmem_limit_bytes=59392 * 1024
        ),
    )(
        attn_ctx,
        o_weight.T,
        residual,
        o_bias,
        post_gain,
        next_gain,
        router_weight.T,
        router_bias.reshape(1, experts),
        routes.T,
        gate_up,
        bias,
        down_weight[0],
        down_bias,
    )
    return (out[:rows].astype(jnp.bfloat16), out[rows:].astype(jnp.bfloat16))


def per_device(
    attn_ctx,
    o_weight,
    o_bias,
    residual,
    post_gain,
    router_weight,
    router_bias,
    routes,
    gate_up_weight,
    gate_up_bias,
    down_weight,
    down_bias,
    next_gain,
):
    req_count = lax.axis_size("req")
    tp_count = lax.axis_size("tp")
    width = o_weight.shape[1]
    tokens_here = attn_ctx.shape[0]
    own_rows = tokens_here // tp_count
    experts = req_count // 2
    top_count = routes.shape[1]
    capacity = min(own_rows, max(2, 2 * top_count * own_rows // experts))
    if capacity == own_rows and req_count == 16 and tp_count == 2 and own_rows % 32 == 0:
        return whole_layer(
            attn_ctx,
            o_weight,
            o_bias,
            residual,
            post_gain,
            router_weight,
            router_bias,
            routes,
            gate_up_weight,
            gate_up_bias,
            down_weight,
            down_bias,
            next_gain,
        )
    own_start = lax.axis_index("tp") * own_rows
    bias_vec = o_bias.astype(jnp.float32)
    proj = jnp.dot(attn_ctx, o_weight, preferred_element_type=jnp.float32).astype(jnp.bfloat16)
    if tp_count == 2:
        theirs = lax.dynamic_slice_in_dim(proj, own_rows - own_start, own_rows, 0)
        mine = lax.dynamic_slice_in_dim(proj, own_start, own_rows, 0)
        arrived = lax.ppermute(theirs, "tp", [(0, 1), (1, 0)])
        summed = mine.astype(jnp.float32) + arrived.astype(jnp.float32)
    else:
        summed = lax.psum_scatter(proj, "tp", scatter_dimension=0, tiled=True).astype(jnp.float32)
    state = (residual.astype(jnp.float32) + summed + bias_vec).astype(jnp.bfloat16)
    own_routes = lax.dynamic_slice_in_dim(routes, own_start, own_rows, 0)
    normed, weights, table = route_rows(
        state, own_routes, post_gain, router_weight, router_bias, experts
    )
    bias_terms = jnp.dot(table, down_bias.astype(jnp.float32), precision=lax.Precision.HIGHEST)
    slots = slot_numbers(own_routes.reshape(1, own_rows * top_count), experts, capacity)
    targets = 2 * own_routes.reshape(-1) * capacity + slots.reshape(-1)
    outgoing = place_rows(normed, targets, capacity, req_count, top_count)
    incoming = lax.all_to_all(outgoing, "req", split_axis=0, concat_axis=0, tiled=True)
    gathered = lax.all_gather(incoming[None], "tp", axis=0, tiled=True).reshape(-1, width)
    sums = lax.psum_scatter(
        expert_apply(gathered, gate_up_weight, gate_up_bias, down_weight).astype(jnp.bfloat16),
        "tp",
        scatter_dimension=0,
        tiled=True,
    ).astype(jnp.float32)
    returned = lax.all_to_all(
        sums.reshape(req_count, capacity, width).astype(jnp.bfloat16),
        "req",
        split_axis=0,
        concat_axis=0,
        tiled=True,
    ).astype(jnp.float32)
    mixed = weigh_parts(returned.reshape(-1, width), targets, capacity, weights, top_count)
    hidden_state = (state.astype(jnp.float32) + mixed + bias_terms).astype(jnp.bfloat16)
    normed_out = rms_norm(hidden_state.astype(jnp.float32), next_gain).astype(jnp.bfloat16)
    return (hidden_state, normed_out)


def solution(mesh):
    return jax.shard_map(
        per_device,
        mesh=mesh,
        in_specs=(
            P("req", "tp"),
            P("tp", None),
            P(),
            P(("req", "tp"), None),
            P(),
            P(),
            P(),
            P("req", None),
            P("req", None, None, "tp"),
            P("req", None, "tp"),
            P("req", "tp", None),
            P(),
            P(),
        ),
        out_specs=(P(("req", "tp"), None), P(("req", "tp"), None)),
        check_vma=False,
    )
```

```python
import functools

import jax
import jax.numpy as jnp
from jax import lax
from jax.experimental import pallas as pl
from jax.experimental.pallas import tpu as pltpu
from jax.sharding import PartitionSpec as P


def rms_norm(values, gain):
    scale = lax.rsqrt(jnp.mean(values * values, axis=-1, keepdims=True) + 1e-05)
    return values * scale * gain.astype(jnp.float32)


def route_rows(state, route_ids, post_gain, router_weight, router_bias, experts):
    normed = rms_norm(state.astype(jnp.float32), post_gain).astype(jnp.bfloat16)
    logits = jnp.dot(normed, router_weight, preferred_element_type=jnp.float32) + router_bias
    onehot = (route_ids[:, :, None] == jnp.arange(experts, dtype=jnp.int32)[None, None, :]).astype(
        jnp.float32
    )
    picked = jnp.sum(onehot * logits[:, None, :], axis=2)
    expo = jnp.exp(picked)
    weights = expo / jnp.sum(expo, axis=1, keepdims=True)
    table = jnp.sum(onehot * weights[:, :, None], axis=1)
    return (normed, weights, table)


def slot_numbers(route_blocks, experts, capacity):
    onehot = (
        route_blocks[:, :, None] == jnp.arange(experts, dtype=jnp.int32)[None, None, :]
    ).astype(jnp.int32)
    earlier = jnp.tril(jnp.ones((onehot.shape[1],) * 2, jnp.float32), -1)
    ranks = jnp.einsum("pq,bqe->bpe", earlier, onehot.astype(jnp.float32)).astype(jnp.int32)
    slots = jnp.sum(ranks * onehot, axis=2)
    offsets = jnp.arange(route_blocks.shape[0], dtype=jnp.int32)[:, None] * capacity
    return slots + offsets


def place_rows(normed, targets, block, req_count, top_count):
    width = normed.shape[1]
    source = jnp.repeat(normed, top_count, axis=0)
    buffer = jnp.zeros((req_count * block, width), jnp.bfloat16)
    index = jnp.concatenate([targets, targets + block])
    buffer = buffer.at[index].set(jnp.concatenate([source, source], axis=0))
    return buffer.reshape(req_count, block, width)


def weigh_parts(flat, targets, block, weights, top_count):
    first = jnp.take(flat, targets, axis=0).astype(jnp.float32)
    second = jnp.take(flat, targets + block, axis=0).astype(jnp.float32)
    values = (first + second) * weights.reshape(-1)[:, None]
    return jnp.sum(values.reshape(-1, top_count, flat.shape[1]), axis=1)


def expert_apply(rows, gate_up_weight, gate_up_bias, down_weight):
    local_width = gate_up_weight.shape[3]
    weight_mat = gate_up_weight[0].reshape(gate_up_weight.shape[1], 2 * local_width)
    projected = jnp.dot(rows, weight_mat, preferred_element_type=jnp.float32)
    projected = projected + gate_up_bias[0].reshape(2 * local_width).astype(jnp.float32)
    gate = jnp.minimum(projected[:, :local_width], 7.0)
    upper = jnp.clip(projected[:, local_width:], -7.0, 7.0)
    act = ((upper + 1.0) * gate * jax.nn.sigmoid(1.702 * gate)).astype(jnp.bfloat16)
    return jnp.dot(act, down_weight[0], preferred_element_type=jnp.float32)


def peer(bits, stride_x):
    req, tp = lax.axis_index("req"), lax.axis_index("tp")
    for bit in (1, 2, 4, 8):
        if bits & bit:
            req = req + bit * (1 - 2 * ((req // bit) % 2))
    return {"req": req, "tp": 1 - tp if stride_x else tp}


GATHER_WIDE = (1,)
SUM_WIDE = (1,)
PLAN = (
    "pre", "own", "ownc", "bias", "ownb", "rx0", "ry0", "wz1", "z1", "s1", "rd0", "z2", "dd0",
    "s2", "w0", "up00", "rx1", "up01", "wd1", "ry1", "up02", "w1", "dn00", "wc1", "dn01",
    "rx2", "ry2", "dn02", "cs00", "z3", "dn03", "rd1", "s3", "ca00", "dd1", "up10", "up11",
    "up12", "rd2", "dn10", "dn11", "dn12", "dn13", "rx3", "dd2", "ry3", "cs10", "cs11", "up20",
    "up21", "ca10", "up22", "dn20", "rd3", "dn21", "dn22", "cs20", "ca11", "dd3", "dn23",
    "cs21", "up30", "ca20", "ha10", "ca21", "up31", "ha20", "up32", "dn30", "ha21", "dn31",
    "cs01", "ha11", "cs30", "za10", "dn32", "dn33", "fa20", "ca30", "ha30", "fa21", "cs31",
    "za11", "ca31", "ca01", "zt11", "fa30", "ha31", "ha00", "zt10", "fa31", "zt30", "zt20",
    "zt21", "ha01", "zt31", "fin",
)


def layer_kernel(
    rows,
    width,
    experts,
    attn_hbm,
    o_weight_ref,
    residual_hbm,
    o_bias_hbm,
    post_gain_hbm,
    next_gain_hbm,
    router_hbm,
    router_bias_hbm,
    routes_hbm,
    gate_up_ref,
    bias_hbm,
    down_ref,
    down_bias_hbm,
    out_ref,
    gathered,
    partial,
    core_in,
    half_in,
    full_in,
    layer_in,
    o_weight,
    gate_up,
    down,
    act,
    attn,
    proj,
    proj_out,
    proj_in,
    padded_rows,
    base,
    attn_ref,
    residual_ref,
    o_bias_ref,
    post_gain_ref,
    next_gain_ref,
    vectors_ref,
    router_ref,
    router_bias_ref,
    routes_ref,
    bias_ref,
    down_bias_ref,
    small_sems,
    load_sems,
    send_sems,
    recv_sems,
):
    half_rows = rows // 2
    hidden = down.shape[0]
    span = 8 * rows
    tail = width // 128 * 128
    req, tp = lax.axis_index("req"), lax.axis_index("tp")
    expert = req // 2
    step_width = 384
    steps = [(start, min(step_width, width - start)) for start in range(0, width, step_width)]
    links = {
        "x": (0, 1),
        "y": (2, 0),
        "c": (1, 0),
        "z1": (4, 0),
        "z2": (8, 0),
        "z3": (12, 0),
    }
    peers = {link: peer(*way) for link, way in links.items()}

    small = [
        pltpu.make_async_copy(source, target, small_sems.at[number])
        for number, (source, target) in enumerate(
            (
                (attn_hbm, attn_ref),
                (residual_hbm, residual_ref),
                (o_bias_hbm, o_bias_ref),
                (post_gain_hbm, post_gain_ref),
                (next_gain_hbm, next_gain_ref),
                (router_hbm, router_ref),
                (router_bias_hbm, router_bias_ref),
                (routes_hbm, routes_ref),
                (bias_hbm, bias_ref),
                (down_bias_hbm, down_bias_ref),
            )
        )
    ]
    small[0].start()
    loads = []
    for number, (start, size) in enumerate(steps):
        here = pl.ds(start, size)
        loads.append(
            pltpu.make_async_copy(o_weight_ref.at[here, :], o_weight.at[here, :], load_sems.at[number])
        )
    loads.append(pltpu.make_async_copy(gate_up_ref, gate_up, load_sems.at[len(steps)]))
    loads.append(pltpu.make_async_copy(down_ref, down, load_sems.at[len(steps) + 1]))
    ahead = 3
    for load in loads[:1] + small[1:] + loads[1:ahead]:
        load.start()
    barrier = pltpu.get_barrier_semaphore()
    for link in peers:
        pl.semaphore_signal(
            barrier, inc=1, device_id=peers[link], device_id_type=pl.DeviceIdType.MESH
        )

    copies = {}

    def send(name, link, source, target):
        number = len(copies)
        copies[name] = pltpu.make_async_remote_copy(
            src_ref=source,
            dst_ref=target,
            send_sem=send_sems.at[number],
            recv_sem=recv_sems.at[number],
            device_id=peers[link],
            device_id_type=pl.DeviceIdType.MESH,
        )
        copies[name].start()

    def arrived(name):
        copies[name].wait_recv()

    def place(layer, core, spot, half=0):
        return ((layer * 2 + core) * 4 + spot) * rows + half * half_rows

    def block(ref, layer, core, spot):
        return ref.at[pl.ds(place(layer, core, spot), rows), :]

    def piece(ref, layer, core, spot, half):
        return ref.at[pl.ds(place(layer, core, spot, half), half_rows), :]

    small[0].wait()
    attn[0:rows, :] = attn_ref[pl.ds(pl.multiple_of(tp * rows, rows), rows), :]
    attn[rows:, :] = attn_ref[pl.ds(pl.multiple_of((1 - tp) * rows, rows), rows), :]
    for number, (start, size) in enumerate(steps):
        loads[number].wait()
        for load in loads[number + ahead : number + ahead + 1]:
            load.start()
        both = lax.dot_general(
            attn[...],
            o_weight[start : start + size, :],
            (((1,), (1,)), ((), ())),
            preferred_element_type=jnp.float32,
        )
        proj[:, start : start + size] = both[0:rows]
        proj_out[:, start : start + size] = both[rows:].astype(jnp.bfloat16)
        if number == 0:
            pl.semaphore_wait(barrier, len(links))
        here = pl.ds(start, size)
        send(("proj", number), "x", proj_out.at[:, here], proj_in.at[:, here])

    def op_pre():
        for load in small[1:]:
            load.wait()
        for number, ref in enumerate((o_bias_ref, post_gain_ref, next_gain_ref)):
            vectors_ref[number : number + 1, :] = ref[...].astype(jnp.float32).reshape(1, width)
        squares = jnp.zeros((rows, 1), jnp.float32)
        for number, (start, size) in enumerate(steps):
            here = slice(start, start + size)
            arrived(("proj", number))
            state = (
                residual_ref[:, here].astype(jnp.float32)
                + (proj[:, here] + proj_in[:, here].astype(jnp.float32))
                + vectors_ref[0:1, here]
            ).astype(jnp.bfloat16).astype(jnp.float32)
            base[:, here] = state
            squares = squares + jnp.sum(state * state, axis=1, keepdims=True)
        scale = lax.rsqrt(squares / width + 1e-05)
        padded_rows[:, tail:] = jnp.zeros((rows, padded_rows.shape[1] - tail), jnp.float32)
        padded_rows[:, 0:width] = base[...] * scale * vectors_ref[1:2, :]
        normed = padded_rows[:, 0:width].astype(jnp.bfloat16)
        logits = (
            lax.dot_general(
                normed,
                router_ref[...],
                (((1,), (1,)), ((), ())),
                preferred_element_type=jnp.float32,
            )
            + router_bias_ref[...]
        )
        given = routes_ref[...].astype(jnp.float32)
        here = (rows, given.shape[1])
        mine = lax.broadcasted_iota(jnp.int32, here, 0) + tp * rows
        mine = (mine == lax.broadcasted_iota(jnp.int32, here, 1)).astype(jnp.float32)
        routes = lax.dot_general(
            mine, given, (((1,), (1,)), ((), ())), preferred_element_type=jnp.float32
        )
        lane = lax.broadcasted_iota(jnp.int32, logits.shape, 1).astype(jnp.float32)
        hit = lane == routes[:, 0:1]
        for number in range(1, routes.shape[1]):
            hit = hit | (lane == routes[:, number : number + 1])
        expo = jnp.where(hit, jnp.exp(logits), 0.0)
        table = expo / jnp.sum(expo, axis=1, keepdims=True)
        high = table.astype(jnp.bfloat16).astype(jnp.float32)
        low = (table - high).astype(jnp.bfloat16).astype(jnp.float32)
        last = padded_rows[:, tail:]
        lane = lax.broadcasted_iota(jnp.int32, last.shape, 1) - (width - tail)
        for number in range(experts):
            last = jnp.where(lane == number, high[:, number : number + 1], last)
            last = jnp.where(lane == number + experts, low[:, number : number + 1], last)
        gathered[0:rows, 0:tail] = padded_rows[:, 0:tail].astype(jnp.bfloat16)
        gathered[0:rows, tail:] = last.astype(jnp.bfloat16)
        padded_rows[:, tail:] = last

    def op_bias():
        last = padded_rows[:, tail:]
        lane = lax.broadcasted_iota(jnp.int32, last.shape, 1) - (width - tail)
        for start, size in steps:
            here = slice(start, start + size)
            total = base[:, here]
            for number in range(experts):
                mine = (lane == number) | (lane == number + experts)
                weight = jnp.sum(jnp.where(mine, last, 0.0), axis=1, keepdims=True)
                total = total + weight * down_bias_ref[number : number + 1, here].astype(jnp.float32)
            base[:, here] = total

    def across(layer, spot):
        send(
            ("c", layer, spot),
            "c",
            block(gathered, layer, 0, spot),
            block(gathered, layer, 1, spot),
        )

    def along(name, link, layer, spot, half, far_layer, far_spot):
        send(
            name, link, piece(gathered, layer, 0, spot, half), piece(gathered, far_layer, 0, far_spot, half)
        )

    def spread(layer):
        if layer in GATHER_WIDE:
            along(("x", layer), "x", layer, 0, 1, layer, 1)
            along(("y", layer), "y", layer, 0, 0, layer, 2)
        else:
            own = block(gathered, layer, 0, 0)
            send(("x", layer), "x", own, block(gathered, layer, 0, 1))
            send(("y", layer), "y", own, block(gathered, layer, 0, 2))
        across(layer, 0)

    def op_own():
        spread(0)

    def op_own2():
        send("z2", "z2", block(gathered, 0, 0, 0), block(gathered, 2, 0, 0))

    def op_own1():
        send("z1", "z1", block(gathered, 0, 0, 0), block(gathered, 1, 0, 0))

    def op_z1():
        arrived("z1")

    def op_z2():
        arrived("z2")
        send("z3", "z1", block(gathered, 2, 0, 0), block(gathered, 3, 0, 0))

    def op_z3():
        arrived("z3")

    def op_rx(layer):
        arrived(("x", layer))
        if layer not in GATHER_WIDE:
            along(("yd", layer), "y", layer, 1, 1, layer, 3)
            across(layer, 1)

    def op_ry(layer):
        arrived(("y", layer))
        if layer not in GATHER_WIDE:
            along(("xd", layer), "x", layer, 2, 0, layer, 3)
            across(layer, 2)

    def op_wz(layer):
        source = 2 if layer == 3 else 0
        link = "z1" if layer == 3 else "z" + str(layer)
        along(("zx", layer), link, source, 1, 0, layer, 1)
        along(("zy", layer), link, source, 2, 1, layer, 2)

    def op_wd(layer):
        arrived(("zx", layer))
        along(("yd", layer), "y", layer, 1, 0, layer, 3)
        arrived(("zy", layer))
        along(("xd", layer), "x", layer, 2, 1, layer, 3)

    def op_wc(layer):
        across(layer, 1)
        across(layer, 2)

    def op_rd(layer):
        arrived(("xd", layer))
        arrived(("yd", layer))
        across(layer, 3)

    def op_dd(layer):
        for spot in range(4):
            arrived(("c", layer, spot))

    for load in loads[len(steps) + ahead :]:
        load.start()

    def op_w(number):
        loads[len(steps) + number].wait()

    def op_up(layer, step):
        here = pl.ds(layer * span, span)
        start = step * 256
        size = min(256, hidden - start)
        sides = []
        for side in range(2):
            sides.append(
                lax.dot_general(
                    gathered[here, 0:width],
                    gate_up[pl.ds(side * hidden + start, size), :],
                    (((1,), (1,)), ((), ())),
                    preferred_element_type=jnp.float32,
                )
                + bias_ref[side : side + 1, start : start + size].astype(jnp.float32)
            )
        gate = jnp.minimum(sides[0], 7.0)
        upper = jnp.clip(sides[1], -7.0, 7.0)
        act[:, start : start + size] = (
            (upper + 1.0) * gate * jax.nn.sigmoid(1.702 * gate)
        ).astype(jnp.bfloat16)

    def op_dn(layer, step):
        here = pl.ds(layer * span, span)
        extra = gathered[here, tail:].astype(jnp.float32)
        lane = lax.broadcasted_iota(jnp.int32, extra.shape, 1) - (width - tail)
        mine = (lane == expert) | (lane == expert + experts)
        share = jnp.sum(jnp.where(mine, extra, 0.0), axis=1, keepdims=True)
        start = step * 768
        size = min(768, width - start)
        partial[here, start : start + size] = (
            jnp.dot(act[...], down[:, start : start + size], preferred_element_type=jnp.float32)
            * share
        ).astype(jnp.bfloat16)

    cut = width // 256 // 2 * 256 + 256
    columns = ((0, cut), (cut, width - cut))

    def op_cs(layer, part):
        here = pl.ds(*columns[part])
        send(
            ("cs", layer, part),
            "c",
            partial.at[pl.ds(place(layer, 1, 0), 4 * rows), here],
            core_in.at[pl.ds(layer * 4 * rows, 4 * rows), here],
        )

    def add(part, start, size, *others):
        left, right = columns[part][0], sum(columns[part])
        if len(others) == 1:
            [(other, first)] = others
            partial[start : start + size, left:right] += other[first : first + size, left:right]
            return
        total = partial[start : start + size, left:right].astype(jnp.float32)
        for other, first in others:
            total = total + other[first : first + size, left:right].astype(jnp.float32)
        partial[start : start + size, left:right] = total.astype(jnp.bfloat16)

    def half_place(layer, side, turn):
        return ((layer * 2 + side) * 2 + turn) * half_rows

    def send_half(part, layer, side, spot, half, turn):
        here = pl.ds(*columns[part])
        send(
            ("xy"[side] + "h", layer, turn, part),
            "xy"[side],
            partial.at[pl.ds(place(layer, 0, spot, half), half_rows), here],
            half_in.at[pl.ds(half_place(layer, side, turn), half_rows), here],
        )

    def add_half(part, layer, side, spot, half, turn):
        arrived(("xy"[side] + "h", layer, turn, part))
        add(part, place(layer, 0, spot, half), half_rows, (half_in, half_place(layer, side, turn)))

    def op_ca(layer, part):
        arrived(("cs", layer, part))
        first = layer * 4 * rows
        wide = layer in SUM_WIDE
        add(part, place(layer, 0, 3), rows, (core_in, first + 3 * rows))
        if wide:
            send_half(part, layer, 0, 3, 1, 0)
            send_half(part, layer, 1, 3, 0, 0)
        else:
            send_half(part, layer, 0, 3, 0, 0)
            send_half(part, layer, 1, 3, 1, 0)
        for spot in (1, 2):
            add(part, place(layer, 0, spot), rows, (core_in, first + spot * rows))
            if wide:
                send_half(part, layer, spot - 1, spot, 2 - spot, 1)
        add(part, place(layer, 0, 0), rows, (core_in, first))

    def op_ha(layer, part):
        here = pl.ds(*columns[part])
        if layer in SUM_WIDE:
            add_half(part, layer, 0, 2, 1, 0)
            add_half(part, layer, 1, 1, 0, 0)
            add_half(part, layer, 0, 0, 1, 1)
            add_half(part, layer, 1, 0, 0, 1)
            for turn, (spot, half, size) in enumerate(((1, 0, 1), (2, 1, 1), (0, 0, 2))):
                target = (layer * 2 - 2) * rows + turn * half_rows
                send(
                    ("zs", layer, turn, part),
                    "z" + str(layer),
                    partial.at[pl.ds(place(layer, 0, spot, half), size * half_rows), here],
                    layer_in.at[pl.ds(target, size * half_rows), here],
                )
            return
        add_half(part, layer, 0, 2, 0, 0)
        add_half(part, layer, 1, 1, 1, 0)
        for side, link in enumerate("xy"):
            send(
                (link + "f", layer, part),
                link,
                partial.at[pl.ds(place(layer, 0, 1 + side), rows), here],
                full_in.at[pl.ds((layer * 2 + side) * rows, rows), here],
            )

    def op_fa(layer, part):
        here = pl.ds(*columns[part])
        first = layer * 2 * rows
        arrived(("xf", layer, part))
        arrived(("yf", layer, part))
        add(part, place(layer, 0, 0), rows, (full_in, first), (full_in, first + rows))
        send(
            ("zs", layer, 2, part),
            "z" + str(layer),
            partial.at[pl.ds(place(layer, 0, 0), rows), here],
            layer_in.at[pl.ds((layer * 2 - 1) * rows, rows), here],
        )

    def op_za(layer, part):
        first = (layer * 2 - 2) * rows
        arrived(("zs", layer, 0, part))
        add(part, place(0, 0, 1, 0), half_rows, (layer_in, first))
        arrived(("zs", layer, 1, part))
        add(part, place(0, 0, 2, 1), half_rows, (layer_in, first + half_rows))

    def op_zt(layer, part):
        left, right = columns[part][0], sum(columns[part])
        first = (layer * 2 - 1) * rows
        arrived(("zs", layer, 2, part))
        base[:, left:right] += layer_in[first : first + rows, left:right].astype(jnp.float32)

    def op_fin():
        base[...] += partial[0:rows, :].astype(jnp.float32)
        squares = jnp.zeros((rows, 1), jnp.float32)
        for part, (left, size) in enumerate(columns):
            here = slice(left, left + size)
            arrived(("xf", 0, part))
            arrived(("yf", 0, part))
            total = base[:, here]
            for first in (0, rows):
                total = total + full_in[first : first + rows, here].astype(jnp.float32)
            total = total.astype(jnp.bfloat16).astype(jnp.float32)
            base[:, here] = total
            out_ref[0:rows, here] = total.astype(jnp.bfloat16)
            squares = squares + jnp.sum(total * total, axis=1, keepdims=True)
        scale = lax.rsqrt(squares / width + 1e-05)
        out_ref[rows:, :] = (base[...] * scale * vectors_ref[2:3, :]).astype(jnp.bfloat16)

    ops = dict(
        pre=op_pre, bias=op_bias, own=op_own, ownb=op_own2, ownc=op_own1, w=op_w, z1=op_z1, z2=op_z2, z3=op_z3,
        s=spread, rx=op_rx, ry=op_ry, wz=op_wz, wd=op_wd, wc=op_wc, rd=op_rd, dd=op_dd, up=op_up,
        dn=op_dn, cs=op_cs, ca=op_ca, ha=op_ha, fa=op_fa, za=op_za, zt=op_zt, fin=op_fin,
    )
    for name in PLAN:
        if name in ops:
            ops[name]()
        else:
            stem = name.rstrip("0123456789")
            ops[stem](*[int(digit) for digit in name[len(stem) :]])
    for copy in copies.values():
        copy.wait_send()


def whole_layer(
    attn_ctx,
    o_weight,
    o_bias,
    residual,
    post_gain,
    router_weight,
    router_bias,
    routes,
    gate_up_weight,
    gate_up_bias,
    down_weight,
    down_bias,
    next_gain,
):
    rows, width = residual.shape
    experts = router_bias.shape[0]
    hidden = down_weight.shape[1]
    padded = (width + 2 * experts + 127) // 128 * 128
    gate_up = jnp.transpose(gate_up_weight[0], (1, 2, 0)).reshape(2 * hidden, width)
    bias = gate_up_bias[0]
    vmem = pl.BlockSpec(memory_space=pltpu.VMEM)
    hbm = pl.BlockSpec(memory_space=pl.ANY)
    copies = 160
    out = pl.pallas_call(
        functools.partial(layer_kernel, rows, width, experts),
        out_shape=jax.ShapeDtypeStruct((2 * rows, width), jnp.bfloat16),
        in_specs=[hbm] * 13,
        out_specs=vmem,
        scratch_shapes=[
            pltpu.VMEM((32 * rows, padded), jnp.bfloat16),
            pltpu.VMEM((32 * rows, width), jnp.bfloat16),
            pltpu.VMEM((16 * rows, width), jnp.bfloat16),
            pltpu.VMEM((8 * rows, width), jnp.bfloat16),
            pltpu.VMEM((8 * rows, width), jnp.bfloat16),
            pltpu.VMEM((6 * rows, width), jnp.bfloat16),
            pltpu.VMEM((width, attn_ctx.shape[1]), jnp.bfloat16),
            pltpu.VMEM((2 * hidden, width), jnp.bfloat16),
            pltpu.VMEM((hidden, width), jnp.bfloat16),
            pltpu.VMEM((8 * rows, hidden), jnp.bfloat16),
            pltpu.VMEM(attn_ctx.shape, jnp.bfloat16),
            pltpu.VMEM((rows, width), jnp.float32),
            pltpu.VMEM((rows, width), jnp.bfloat16),
            pltpu.VMEM((rows, width), jnp.bfloat16),
            pltpu.VMEM((rows, padded), jnp.float32),
            pltpu.VMEM((rows, width), jnp.float32),
            pltpu.VMEM(attn_ctx.shape, jnp.bfloat16),
            pltpu.VMEM((rows, width), jnp.bfloat16),
            pltpu.VMEM((width,), jnp.bfloat16),
            pltpu.VMEM((width,), jnp.bfloat16),
            pltpu.VMEM((width,), jnp.bfloat16),
            pltpu.VMEM((3, width), jnp.float32),
            pltpu.VMEM((experts, width), jnp.bfloat16),
            pltpu.VMEM((1, experts), jnp.float32),
            pltpu.VMEM(routes.shape[::-1], jnp.int32),
            pltpu.VMEM((2, hidden), jnp.bfloat16),
            pltpu.VMEM((experts, width), jnp.bfloat16),
            pltpu.SemaphoreType.DMA((10,)),
            pltpu.SemaphoreType.DMA((16,)),
            pltpu.SemaphoreType.DMA((copies,)),
            pltpu.SemaphoreType.DMA((copies,)),
        ],
        compiler_params=pltpu.CompilerParams(
            collective_id=0, has_side_effects=True, vmem_limit_bytes=59392 * 1024
        ),
    )(
        attn_ctx,
        o_weight.T,
        residual,
        o_bias,
        post_gain,
        next_gain,
        router_weight.T,
        router_bias.reshape(1, experts),
        routes.T,
        gate_up,
        bias,
        down_weight[0],
        down_bias,
    )
    return (out[:rows], out[rows:])


def per_device(
    attn_ctx,
    o_weight,
    o_bias,
    residual,
    post_gain,
    router_weight,
    router_bias,
    routes,
    gate_up_weight,
    gate_up_bias,
    down_weight,
    down_bias,
    next_gain,
):
    req_count = lax.axis_size("req")
    tp_count = lax.axis_size("tp")
    width = o_weight.shape[1]
    tokens_here = attn_ctx.shape[0]
    own_rows = tokens_here // tp_count
    experts = req_count // 2
    top_count = routes.shape[1]
    capacity = min(own_rows, max(2, 2 * top_count * own_rows // experts))
    if capacity == own_rows and req_count == 16 and tp_count == 2 and own_rows % 32 == 0:
        return whole_layer(
            attn_ctx,
            o_weight,
            o_bias,
            residual,
            post_gain,
            router_weight,
            router_bias,
            routes,
            gate_up_weight,
            gate_up_bias,
            down_weight,
            down_bias,
            next_gain,
        )
    own_start = lax.axis_index("tp") * own_rows
    bias_vec = o_bias.astype(jnp.float32)
    proj = jnp.dot(attn_ctx, o_weight, preferred_element_type=jnp.float32).astype(jnp.bfloat16)
    if tp_count == 2:
        theirs = lax.dynamic_slice_in_dim(proj, own_rows - own_start, own_rows, 0)
        mine = lax.dynamic_slice_in_dim(proj, own_start, own_rows, 0)
        arrived = lax.ppermute(theirs, "tp", [(0, 1), (1, 0)])
        summed = mine.astype(jnp.float32) + arrived.astype(jnp.float32)
    else:
        summed = lax.psum_scatter(proj, "tp", scatter_dimension=0, tiled=True).astype(jnp.float32)
    state = (residual.astype(jnp.float32) + summed + bias_vec).astype(jnp.bfloat16)
    own_routes = lax.dynamic_slice_in_dim(routes, own_start, own_rows, 0)
    normed, weights, table = route_rows(
        state, own_routes, post_gain, router_weight, router_bias, experts
    )
    bias_terms = jnp.dot(table, down_bias.astype(jnp.float32), precision=lax.Precision.HIGHEST)
    slots = slot_numbers(own_routes.reshape(1, own_rows * top_count), experts, capacity)
    targets = 2 * own_routes.reshape(-1) * capacity + slots.reshape(-1)
    outgoing = place_rows(normed, targets, capacity, req_count, top_count)
    incoming = lax.all_to_all(outgoing, "req", split_axis=0, concat_axis=0, tiled=True)
    gathered = lax.all_gather(incoming[None], "tp", axis=0, tiled=True).reshape(-1, width)
    sums = lax.psum_scatter(
        expert_apply(gathered, gate_up_weight, gate_up_bias, down_weight).astype(jnp.bfloat16),
        "tp",
        scatter_dimension=0,
        tiled=True,
    ).astype(jnp.float32)
    returned = lax.all_to_all(
        sums.reshape(req_count, capacity, width).astype(jnp.bfloat16),
        "req",
        split_axis=0,
        concat_axis=0,
        tiled=True,
    ).astype(jnp.float32)
    mixed = weigh_parts(returned.reshape(-1, width), targets, capacity, weights, top_count)
    hidden_state = (state.astype(jnp.float32) + mixed + bias_terms).astype(jnp.bfloat16)
    normed_out = rms_norm(hidden_state.astype(jnp.float32), next_gain).astype(jnp.bfloat16)
    return (hidden_state, normed_out)


def solution(mesh):
    return jax.shard_map(
        per_device,
        mesh=mesh,
        in_specs=(
            P("req", "tp"),
            P("tp", None),
            P(),
            P(("req", "tp"), None),
            P(),
            P(),
            P(),
            P("req", None),
            P("req", None, None, "tp"),
            P("req", None, "tp"),
            P("req", "tp", None),
            P(),
            P(),
        ),
        out_specs=(P(("req", "tp"), None), P(("req", "tp"), None)),
        check_vma=False,
    )
```
